128 devices in a mesh: cls: 8 (over y, core), mem: 16 (over z, x).
Axes of the slice: x: 4, y: 4, z: 4, core: 2. Of those that a mesh axis runs over, the one named last changes fastest.
Arguments:
- images: bfloat16 [3072, 65536], P(('cls', 'mem')), may hold values from -6 to 6
- owner_group: int32 [3072, 1], P(('cls', 'mem')), may hold values from 0 to 7; in each aligned block of 24 rows (0 to 23, 24 to 47, ...) at most 6 rows name the same one
- bin_in_group: int32 [3072], P(('cls', 'mem')), may hold values from 0 to 7
- defocus: bfloat16 [3072], P(('cls', 'mem')), may hold values from 0.5 to 2
- projections: bfloat16 [64, 65536], P('cls'), may hold values from -6 to 6
- sketch_weight: bfloat16 [64, 48], replicated, may hold values from -0.875 to 0.875
Outputs:
- basis: bfloat16 [8, 64, 65536], P('cls', None, 'mem')
The draws below stay inside these ranges and needn't reach their ends.
Inputs may be any that keep to these rules, and one draw needn't show every extreme that they name: `owner_group`: in the particles of one device no class group is named more than 6 times, and 6 is reached on some device.
All inputs are finite; a program needn't handle non-finite values.
Results may differ from the reference program's by a relative error of at most 0.012.
The reference program's roundings to bfloat16 on the way count: a program that leaves them out, or rounds other values in their place, can miss the bound.
Values may be sent and summed in bfloat16 or wider, within the bound.
A program may use at most 128 MiB of HBM per device.

```python
import math
import jax
import jax.numpy as jnp
import numpy as np
from jax import lax

SIDE = 256
K = 64
P_DEV = 24
CAP = 6
BIN_CLS = 8
PIX = 65536
SLOTS = 48
BINS = 64
PARTICLES = 3072
N_CLS = 8
N_MEM = 16


def with_ends(drawn, own_key, low, high):
    longest = drawn.shape.index(max(drawn.shape))
    spots = []
    for shift in (0, 1):
        where = [jax.random.randint(jax.random.fold_in(own_key, axis), (), 0, length) for axis, length in enumerate(drawn.shape)]
        where[longest] = (where[longest] + shift) % drawn.shape[longest]
        spots.append(tuple(where))
    return drawn.at[spots[0]].set(low).at[spots[1]].set(high)


def block_levels(rng, dims, shards, least, top_value):
    def one(axis_at, parts):
        heights = jax.random.uniform(jax.random.fold_in(jax.random.fold_in(rng, 6), axis_at), (parts,), jnp.float32, least / len(shards), top_value / len(shards))
        return jnp.repeat(jnp.exp(heights), dims[axis_at] // parts).reshape((-1,) + (1,) * (len(dims) - axis_at - 1))

    factor_of = one(*shards[0])
    for cut in shards[1:]:
        factor_of = factor_of * one(*cut)
    return factor_of


def deal_out(stream_key, own, number, rows, number_of, top, limit, skew):
    sequence = jax.random.permutation(stream_key, number_of)
    packed, ordinary = load_shares(number_of, rows * top, limit, skew, True), load_shares(number_of, rows * top, limit, skew, False)
    places = jnp.arange(number_of)

    def named(tallies, turn):
        used = int((tallies > 0).sum())
        fixed = max(1, used // 4)
        shifted = fixed + (places - fixed + turn * (used - fixed)) % max(1, number_of - fixed)
        return jnp.zeros((number_of,), jnp.int32).at[sequence[jnp.where(places < fixed, places, shifted)]].set(jnp.asarray(tallies, jnp.int32))

    tallies = jnp.where(number % 4 == 0, named(packed, number // 4), named(ordinary, number - number // 4 - 1))
    mixed = jax.random.permutation(jax.random.fold_in(own, 3), number_of)
    donor, taker = mixed[0:number_of // 2 * 2:2], mixed[1:number_of // 2 * 2:2]
    slack = jnp.minimum(tallies[donor] - 1, limit - tallies[taker]) // 2
    slack = jnp.where((donor == sequence[0]) | (taker == sequence[0]) | (tallies[taker] == 0), 0, jnp.maximum(slack, 0))
    shifted = jax.random.randint(jax.random.fold_in(own, 4), (number_of // 2,), 0, 1 << 20) % (slack + 1)
    tallies = tallies.at[donor].add(-shifted).at[taker].add(shifted)
    items = jnp.searchsorted(jnp.cumsum(tallies), jnp.arange(rows * top), side="right").astype(jnp.int32)
    listing = items.reshape(top, rows).T
    listing = listing[jax.random.permutation(jax.random.fold_in(own, 1), rows)]
    turn = jax.random.randint(jax.random.fold_in(own, 2), (rows, 1), 0, top)
    return jnp.take_along_axis(listing, (jnp.arange(top)[None, :] + turn) % top, axis=1)


def load_shares(count, total, limit, slope, full):
    weights = [(1 << 20) // math.isqrt(standing ** slope) + 1 for standing in range(1, count + 1)]
    largest = limit if full else min(limit, max(-(-total // count), total * weights[0] // sum(weights)))
    least = 1 if total - largest >= count - 1 else 0
    counts, rest = [largest] + [least] * (count - 1), total - largest - least * (count - 1)
    while rest > 0:
        free = [i for i in range(1, count) if counts[i] < largest] or [i for i in range(1, count) if counts[i] < limit]
        mass, left = sum([weights[i] for i in free]), rest
        for i in free:
            extra = min(limit - counts[i], max(1, left * weights[i] // mass), rest)
            counts[i] = counts[i] + extra
            rest = rest - extra
    return np.array(counts)


def scatter_about(rng, shape, spread, most, split=(), held_as=jnp.bfloat16):
    drawn = jax.random.normal(rng, shape, jnp.float32) * spread
    if len(split) > 0:
        drawn = block_levels(rng, shape, split, -0.22, 0.18) * drawn
    return jnp.clip(drawn, min=-most, max=most).astype(held_as)


def setup_inputs(seed: int = 0) -> dict:
    seeds = jax.random.split(jax.random.key(seed), 7)
    images = scatter_about(seeds[0], (PARTICLES, PIX), 1.0, 6.0, ((0, 128),))
    owner_group_keys = jax.random.split(jax.random.fold_in(seeds[1], 1), PARTICLES // P_DEV)
    owner_group_turns = jax.random.permutation(jax.random.fold_in(seeds[1], 3), PARTICLES // P_DEV)
    owner_group = jax.vmap(lambda own, number: deal_out(jax.random.fold_in(seeds[1], 2), own, number, P_DEV, N_CLS, 1, CAP, 2))(owner_group_keys, owner_group_turns).reshape((PARTICLES, 1))
    bin_in_group = with_ends(jax.random.randint(seeds[2], (PARTICLES,), 0, BIN_CLS), jax.random.fold_in(seeds[2], 1), 0, BIN_CLS - 1).astype(jnp.int32)
    defocus = jnp.clip(jnp.exp(math.log(2.0) - 1.3862944 * jax.random.uniform(seeds[3], (PARTICLES,), jnp.float32) ** block_levels(seeds[3], (PARTICLES,), ((0, 128),), -0.2, 0.2)), 0.5, 2.0).astype(jnp.bfloat16)
    projections = scatter_about(seeds[4], (BINS, PIX), 1.0, 6.0, ((0, 8),))
    sketch_weight = scatter_about(seeds[5], (K, SLOTS), SLOTS ** -0.5, 0.875)
    return dict(images=images, owner_group=owner_group, bin_in_group=bin_in_group, defocus=defocus, projections=projections, sketch_weight=sketch_weight)


def wave_grid(side):
    position = jnp.arange(side * side, dtype=jnp.int32)
    column = position % side
    row_idx = position // side
    fx = jnp.where(column < side // 2, column, column - side).astype(jnp.float32) / side
    fy = jnp.where(row_idx < side // 2, row_idx, row_idx - side).astype(jnp.float32) / side
    return 160.0 * (fx * fx + fy * fy)

def norm_basis(matrix):
    gram = jnp.dot(matrix, matrix.T, preferred_element_type=jnp.float32)
    total = jnp.trace(gram) + 1e-06
    scaled = gram / total
    ident = jnp.eye(gram.shape[0], dtype=jnp.float32)
    first = 1.5 * ident - 0.5 * scaled
    later = jnp.dot(jnp.dot(first, scaled, precision=lax.Precision.HIGHEST), first, precision=lax.Precision.HIGHEST)
    second = 1.5 * ident - 0.5 * later
    coef = jnp.dot(second, first, precision=lax.Precision.HIGHEST) * jnp.sqrt(PIX / total)
    coef = coef.astype(jnp.bfloat16)
    return jnp.dot(coef, matrix, preferred_element_type=jnp.float32).astype(jnp.bfloat16)

def reference(images, owner_group, bin_in_group, defocus, projections, sketch_weight):
    owners = owner_group[:, 0].reshape(N_CLS, N_MEM, P_DEV)
    onehot = (owners[..., None] == jnp.arange(N_CLS, dtype=jnp.int32)).astype(jnp.int32)
    before = jnp.cumsum(onehot, axis=2) - onehot
    rank = lax.optimization_barrier(jnp.sum(onehot * before, axis=3))
    images4 = images.reshape(N_CLS, N_MEM, P_DEV, PIX)
    bins3 = bin_in_group.reshape(N_CLS, N_MEM, P_DEV)
    focus3 = defocus.reshape(N_CLS, N_MEM, P_DEV)
    grid = wave_grid(SIDE)
    s_index = jnp.arange(N_CLS, dtype=jnp.int32)[:, None, None]
    m_index = jnp.arange(N_MEM, dtype=jnp.int32)[None, :, None]
    slot_ids = jnp.arange(CAP, dtype=jnp.int32)
    levels = N_MEM.bit_length() - 1

    def one_group(group):
        select = (owners[:, :, None, :] == group) & (rank[:, :, None, :] == slot_ids[None, None, :, None])
        source = lax.optimization_barrier(jnp.sum(select.astype(jnp.int32) * jnp.arange(P_DEV, dtype=jnp.int32), axis=3)).astype(jnp.int32)
        valid = jnp.any(select, axis=3)
        picked = images4[s_index, m_index, source]
        picked = jnp.where(valid[..., None], picked, jnp.zeros_like(picked))
        focus = jnp.where(valid, focus3[s_index, m_index, source].astype(jnp.float32), 0.0)
        local_bin = bins3[s_index, m_index, source]
        picked = picked.transpose(1, 0, 2, 3).reshape(N_MEM, SLOTS, PIX)
        focus = focus.transpose(1, 0, 2).reshape(N_MEM, SLOTS)
        valid = valid.transpose(1, 0, 2).reshape(N_MEM, SLOTS)
        local_bin = local_bin.transpose(1, 0, 2).reshape(N_MEM, SLOTS)
        group_proj = lax.dynamic_slice_in_dim(projections, (group * BIN_CLS).astype(jnp.int32), BIN_CLS, 0)
        chosen = group_proj[local_bin].astype(jnp.float32)
        chosen = jnp.where(valid[..., None], chosen, 0.0)
        chi = focus[..., None] * grid
        ctf = -(jnp.sin(chi) + 0.1 * jnp.cos(chi))
        residual = (picked.astype(jnp.float32) - ctf * chosen).astype(jnp.bfloat16)
        sketch = jnp.einsum('ks,msp->mkp', sketch_weight.astype(jnp.float32), residual.astype(jnp.float32)).astype(jnp.bfloat16)
        factors = jax.vmap(norm_basis)(sketch)
        for level in range(levels):
            pairs = factors.reshape(factors.shape[0] // 2, 2, K, PIX)
            joined = (pairs[:, 0].astype(jnp.float32) + pairs[:, 1].astype(jnp.float32)).astype(jnp.bfloat16)
            factors = jax.vmap(norm_basis)(joined)
        return factors[0]
    return lax.map(one_group, jnp.arange(N_CLS, dtype=jnp.int32))
```

```python
import math

import jax
import jax.numpy as jnp
from jax import lax
from jax.sharding import PartitionSpec as P

SIDE = 256
CAP = 6
HI = lax.Precision.HIGHEST


def wave_slice(first, width):
    position = first + jnp.arange(width, dtype=jnp.int32)
    column = position % SIDE
    row_idx = position // SIDE
    fx = jnp.where(column < SIDE // 2, column, column - SIDE).astype(jnp.float32) / SIDE
    fy = jnp.where(row_idx < SIDE // 2, row_idx, row_idx - SIDE).astype(jnp.float32) / SIDE
    return 160.0 * (fx * fx + fy * fy)


def bmm(a, b):
    return jnp.einsum("nij,njk->nik", a, b, precision=HI)


def coefficients(gram, pixels):
    total = jnp.trace(gram, axis1=1, axis2=2)[:, None, None] + 1e-06
    scaled = gram / total
    ident = jnp.eye(gram.shape[1], dtype=jnp.float32)[None]
    first = 1.5 * ident - 0.5 * scaled
    later = bmm(bmm(first, scaled), first)
    second = 1.5 * ident - 0.5 * later
    return bmm(second, first) * jnp.sqrt(pixels / total)


def tree(gram, n_mem, rank, pixels):
    blocks = n_mem
    k = gram.reshape(n_mem, rank, n_mem, rank)
    chain = None
    while True:
        diag = jnp.stack([k[i, :, i, :] for i in range(blocks)])
        c = coefficients(diag, pixels)
        if chain is None:
            chain = c[:, :, None, :]
        else:
            chain = jnp.einsum("nij,njmk->nimk", c, chain, precision=HI)
        if blocks == 1:
            return chain.reshape(rank, n_mem * rank)
        k = jnp.einsum("aij,ajbk->aibk", c, k, precision=HI)
        k = jnp.einsum("aibk,blk->aibl", k, c, precision=HI)
        half = blocks // 2
        k = k.reshape(half, 2, rank, half, 2, rank).sum(axis=(1, 4))
        chain = chain.reshape(half, 2, rank, -1, rank).transpose(0, 2, 1, 3, 4).reshape(half, rank, -1, rank)
        blocks = half


def body(images, owner_group, bin_in_group, defocus, projections, sketch_weight):
    n_cls = lax.axis_size("cls")
    n_mem = lax.axis_size("mem")
    pixels = images.shape[1]
    width = pixels // n_mem
    member = lax.axis_index("mem")
    cls = lax.axis_index("cls")
    p_dev = images.shape[0]
    bins_here = projections.shape[0]
    rank_k = sketch_weight.shape[0]
    owners = owner_group[:, 0]
    onehot = (owners[:, None] == jnp.arange(n_cls, dtype=jnp.int32)[None, :]).astype(jnp.int32)
    before = jnp.cumsum(onehot, axis=0) - onehot
    rank = jnp.sum(onehot * before, axis=1)
    target = owners * CAP + rank
    meta = jnp.stack([target.astype(jnp.float32), defocus.astype(jnp.float32), bin_in_group.astype(jnp.float32)])
    meta = lax.all_gather(meta, ("cls", "mem"), tiled=False).reshape(n_cls, n_mem, 3, p_dev)
    rows = lax.all_to_all(images, "mem", split_axis=1, concat_axis=0, tiled=True)
    rows = rows.reshape(n_mem, p_dev, width)
    mine = lax.dynamic_index_in_dim(meta, cls, 0, keepdims=False)[:, 0]
    select = jnp.arange(n_cls * CAP, dtype=jnp.float32)[None, :, None] == mine[:, None, :]
    sent = jnp.einsum("mti,mip->mtp", select.astype(jnp.bfloat16), rows, preferred_element_type=jnp.float32).astype(jnp.bfloat16)
    sent = sent.reshape(n_mem, n_cls, CAP, width).transpose(1, 0, 2, 3).reshape(n_cls * n_mem * CAP, width)
    got = lax.all_to_all(sent, "cls", split_axis=0, concat_axis=0, tiled=True)
    slot = (cls * CAP + jnp.arange(CAP, dtype=jnp.int32)).astype(jnp.float32)
    pick = (slot[None, None, :, None] == meta[:, :, None, 0, :]).astype(jnp.float32)
    focus = jnp.sum(pick * meta[:, :, None, 1, :], axis=-1).reshape(-1)
    local_bin = jnp.sum(pick * meta[:, :, None, 2, :], axis=-1)
    valid = jnp.sum(pick, axis=-1)
    bins = jnp.arange(bins_here, dtype=jnp.float32)
    table = jnp.where((local_bin[..., None] == bins) & (valid[..., None] > 0.5), 1.0, 0.0)
    table = table.reshape(-1, bins_here).astype(jnp.bfloat16)
    proj = lax.dynamic_slice_in_dim(projections, member * width, width, 1)
    chosen = jnp.dot(table, proj, preferred_element_type=jnp.float32)
    chi = focus[:, None] * wave_slice(member * width, width)[None, :]
    ctf = -math.sqrt(1.01) * jnp.sin(chi + math.atan(0.1))
    residual = (got.astype(jnp.float32) - ctf * chosen).astype(jnp.bfloat16)
    residual = residual.reshape(n_cls, n_mem, CAP, width).transpose(1, 0, 2, 3).reshape(n_mem, n_cls * CAP, width)
    sketch = jnp.einsum("ks,msp->mkp", sketch_weight, residual, preferred_element_type=jnp.float32).astype(jnp.bfloat16)
    sketch = sketch.reshape(n_mem * rank_k, width)
    gram = jnp.einsum("ap,bp->ab", sketch, sketch, preferred_element_type=jnp.float32)
    gram = lax.psum(gram, "mem")
    coef = tree(gram, n_mem, rank_k, float(pixels)).astype(jnp.bfloat16)
    result = jnp.dot(coef, sketch, preferred_element_type=jnp.float32).astype(jnp.bfloat16)
    return result[None]


def solution(mesh):
    in_specs = (
        P(("cls", "mem"), None),
        P(("cls", "mem"), None),
        P(("cls", "mem")),
        P(("cls", "mem")),
        P("cls", None),
        P(),
    )
    out_specs = P("cls", None, "mem")
    return jax.shard_map(body, mesh=mesh, in_specs=in_specs, out_specs=out_specs, check_vma=False)
```

```python
import functools
import math

import jax
import jax.numpy as jnp
import numpy as np
from jax import lax
from jax.experimental import pallas as pl
from jax.experimental.pallas import tpu as pltpu
from jax.sharding import PartitionSpec as P

SIDE = 256
CAP = 6
HI = lax.Precision.HIGHEST
N_CLS = 8
N_MEM = 16
RANK = 64
P_DEV = 24
P_PAD = 32
PIX = 65536
WIDTH = PIX // N_MEM
CHUNKS = 8
W = WIDTH // CHUNKS
PART = N_MEM * CAP
SLOTS = N_CLS * PART
ROWS = N_MEM * RANK
COLS = N_MEM * P_PAD
BLOCK = 256
PAIRS = [(i, j) for i in range(ROWS // BLOCK) for j in range(i, ROWS // BLOCK)]


def sine_terms():
    nodes = np.cos(np.pi * (np.arange(400) + 0.5) / 400) * 0.5
    basis = np.stack([nodes ** (2 * i + 1) for i in range(6)], axis=1)
    wanted = -math.sqrt(1.01) * np.sin(2 * np.pi * nodes)
    return [float(v) for v in np.linalg.lstsq(basis, wanted, rcond=None)[0]]


SINE = sine_terms()


def exchange_kernel(images, meta, proj, weight, spread, s_out, k_out, x_buf, m_buf, sel, send, recv, relay, smeta, rmeta, lmeta,
                    pj, wt, focus, table, grid_q, res, s_buf, acc,
                    xs, xr, ms, mr, ys, yr, fs, ls, lr, pm, os):
    cls = lax.axis_index("cls")
    mem = lax.axis_index("mem")
    y, core = cls // 2, cls % 2
    up, down, far = (y + 1) % 4, (y + 3) % 4, (y + 2) % 4
    z, x = mem // 4, mem % 4

    barrier = pltpu.get_barrier_semaphore()

    def peer(o):
        return ((z + o // 4) % 4) * 4 + (x + o % 4) % 4

    x_buf[...] = jnp.zeros_like(x_buf)
    m_buf[...] = jnp.zeros_like(m_buf)

    @pl.loop(1, N_MEM)
    def _(o):
        pl.semaphore_signal(barrier, inc=1, device_id={"mem": peer(o)}, device_id_type=pl.DeviceIdType.MESH)

    near = [up * 2, up * 2 + 1, down * 2, down * 2 + 1, y * 2 + 1 - core]
    for other in near:
        pl.semaphore_signal(barrier, inc=1, device_id={"cls": other}, device_id_type=pl.DeviceIdType.MESH)

    pl.semaphore_wait(barrier, N_MEM - 1 + len(near))

    def rows_of(ref, member):
        return ref.at[pl.ds(pl.multiple_of(member * P_PAD, P_PAD), P_DEV), :]

    def meta_copy(o, owner):
        return pltpu.make_async_remote_copy(
            src_ref=meta, dst_ref=rows_of(m_buf, owner), send_sem=ms.at[o], recv_sem=mr.at[owner],
            device_id={"mem": peer(o)}, device_id_type=pl.DeviceIdType.MESH)

    def image_part(q, target):
        return images.at[:, pl.ds(pl.multiple_of(target * WIDTH + q * W, W), W)]

    def image_copy(q, o, owner):
        return pltpu.make_async_remote_copy(
            src_ref=image_part(q, peer(o)), dst_ref=rows_of(x_buf.at[q], owner),
            send_sem=xs.at[q, o], recv_sem=xr.at[q, owner],
            device_id={"mem": peer(o)}, device_id_type=pl.DeviceIdType.MESH)

    def own_image(q):
        return pltpu.make_async_copy(image_part(q, mem), rows_of(x_buf.at[q], mem), xs.at[q, 0])

    own_meta = pltpu.make_async_copy(meta, rows_of(m_buf, mem), ms.at[0])
    own_meta.start()

    @pl.loop(1, N_MEM)
    def _(o):
        meta_copy(o, mem).start()

    @pl.loop(0, CHUNKS)
    def _(q):
        own_image(q).start()

        @pl.loop(1, N_MEM)
        def _(o):
            image_copy(q, o, mem).start()

    own_proj = pltpu.make_async_copy(proj.at[:, pl.ds(pl.multiple_of(mem * WIDTH, WIDTH), WIDTH)], pj, pm)
    own_proj.start()

    wide = jnp.dot(weight[...], spread[...], preferred_element_type=jnp.float32)
    column = lax.broadcasted_iota(jnp.int32, (RANK, SLOTS), 1).astype(jnp.float32)
    local = column - PART * jnp.floor((column + 0.5) * (1.0 / PART))
    holder = jnp.floor((local + 0.5) * (1.0 / CAP))
    for m in range(N_MEM):
        wt[m * RANK:(m + 1) * RANK, :] = jnp.where(holder == float(m), wide, 0.0).astype(jnp.bfloat16)

    @pl.loop(0, CHUNKS)
    def _(q):
        place = mem * WIDTH + q * W + lax.broadcasted_iota(jnp.int32, (8, W), 1)
        col = place & (SIDE - 1)
        row = lax.shift_right_logical(place, 8)
        fx = jnp.where(col < SIDE // 2, col, col - SIDE).astype(jnp.float32) * (1.0 / SIDE)
        fy = jnp.where(row < SIDE // 2, row, row - SIDE).astype(jnp.float32) * (1.0 / SIDE)
        grid_q[q] = (fx * fx + fy * fy) * (160.0 / (2 * math.pi))

    acc[...] = jnp.zeros_like(acc)

    own_meta.wait()

    @pl.loop(1, N_MEM)
    def _(o):
        owner = peer(N_MEM - o)
        meta_copy(o, peer(o)).wait_recv()

    lane = lax.broadcasted_iota(jnp.int32, (8, 128), 1)
    third = jnp.where(lane == 3, 1.0, 0.0).astype(jnp.bfloat16)
    code = lax.dot_general(third, m_buf[...], (((1,), (1,)), ((), ())), preferred_element_type=jnp.float32)
    which = lax.shift_right_logical(lax.broadcasted_iota(jnp.int32, (1, COLS), 1), 5).astype(jnp.float32)
    code = code[0:1, :] + 64.0 * which
    item = lax.broadcasted_iota(jnp.int32, (PART, COLS), 0).astype(jnp.float32)
    whose = jnp.floor((item + 0.5) * (1.0 / CAP))
    base = whose * 64.0 + (item - CAP * whose) + 1.0 - code
    for c in range(N_CLS):
        sel[c * PART:(c + 1) * PART, :] = jnp.where(base == -float(c * CAP), 1.0, 0.0).astype(jnp.bfloat16)

    def part_of(ref, group):
        return ref.at[pl.ds(pl.multiple_of(group * PART, PART), PART), :]

    def y_copies(src, dst, mid, sems, rsems, msems, mrsems):
        def remote(a, b, s, r, target):
            return pltpu.make_async_remote_copy(src_ref=a, dst_ref=b, send_sem=s, recv_sem=r,
                                                device_id={"cls": target}, device_id_type=pl.DeviceIdType.MESH)
        here = part_of(dst, cls)
        first = [
            remote(part_of(src, far * 2), mid.at[0], msems.at[0], mrsems.at[0], up * 2 + core),
            remote(part_of(src, far * 2 + 1), mid.at[1], msems.at[1], mrsems.at[1], down * 2 + core),
        ]
        direct = [remote(part_of(src, other), here, sems.at[i], rsems.at[cls], other) for i, other in enumerate(near)]
        own = pltpu.make_async_copy(part_of(src, cls), here, rsems.at[cls])
        again = [
            remote(mid.at[0], part_of(dst, down * 2 + core), sems.at[5], rsems.at[down * 2 + core], up * 2),
            remote(mid.at[1], part_of(dst, up * 2 + core), sems.at[6], rsems.at[up * 2 + core], down * 2 + 1),
        ]
        return first, direct, own, again

    def arrivals(dst, sems, rsems):
        def wait(source):
            pltpu.make_async_remote_copy(
                src_ref=part_of(dst, source), dst_ref=part_of(dst, source), send_sem=sems.at[0], recv_sem=rsems.at[source],
                device_id={"cls": up * 2}, device_id_type=pl.DeviceIdType.MESH).wait_recv()
        for other in near + [far * 2, far * 2 + 1]:
            wait(other)

    metas = y_copies(smeta, rmeta, lmeta, ys.at[CHUNKS], yr.at[CHUNKS], ls.at[CHUNKS], lr.at[CHUNKS])
    smeta[...] = jnp.dot(sel[...], m_buf[...], preferred_element_type=jnp.float32).astype(jnp.bfloat16)
    for copy in metas[0] + metas[1] + [metas[2]]:
        copy.start()

    def chunk_copies(q):
        return y_copies(send.at[q], recv.at[q], relay.at[q], ys.at[q], yr.at[q], ls.at[q], lr.at[q])

    def sort(q):
        own_image(q).wait()

        @pl.loop(1, N_MEM)
        def _(o):
            image_copy(q, o, peer(o)).wait_recv()

        send[q] = jnp.dot(sel[...], x_buf[q], preferred_element_type=jnp.float32).astype(jnp.bfloat16)
        first, direct, own, _ = chunk_copies(q)
        for copy in first + direct + [own]:
            copy.start()

    def forward(copies):
        first, _, _, again = copies
        for a, b in zip(first, again):
            a.wait_recv()
            b.start()

    def prepare():
        metas[2].wait()
        arrivals(rmeta, ys.at[CHUNKS], yr.at[CHUNKS])
        pick = lax.broadcasted_iota(jnp.int32, (128, 128), 0)
        m = rmeta[...]
        def lanes(i):
            return jnp.dot(m, jnp.where(pick == i, 1.0, 0.0).astype(jnp.bfloat16), preferred_element_type=jnp.float32)
        focus[...] = lanes(0)
        at = lax.broadcasted_iota(jnp.int32, (SLOTS, 128), 1).astype(jnp.float32)
        table[...] = jnp.where((lanes(1) == at) & (lanes(2) == 1.0), 1.0, 0.0).astype(jnp.bfloat16)
        own_proj.wait()

    def consume(q):
        _, _, own, _ = chunk_copies(q)
        own.wait()
        arrivals(recv.at[q], ys.at[q], yr.at[q])
        projected = pj[:, pl.ds(pl.multiple_of(q * W, W), W)]

        @pl.loop(0, SLOTS // 16)
        def _(i):
            r = pl.ds(pl.multiple_of(i * 16, 16), 16)
            chosen = jnp.dot(table[r, 0:8], projected, preferred_element_type=jnp.float32)
            f = focus[r, :]
            for l in range(W // 128):
                cols = slice(l * 128, (l + 1) * 128)
                g = grid_q[q, :, cols]
                turn = f * jnp.concatenate([g, g], axis=0) + math.atan(0.1) / (2 * math.pi)
                turn = turn - jnp.round(turn)
                sq = turn * turn
                value = SINE[5]
                for term in SINE[4::-1]:
                    value = value * sq + term
                ctf = value * turn
                got = recv[q, r, cols].astype(jnp.float32)
                res[r, cols] = (got - ctf * chosen[:, cols]).astype(jnp.bfloat16)

        s_buf[q] = jnp.dot(wt[...], res[...], preferred_element_type=jnp.float32).astype(jnp.bfloat16)
        for n, (i, j) in enumerate(PAIRS):
            acc[n] += lax.dot_general(
                s_buf[q, i * BLOCK:(i + 1) * BLOCK, :], s_buf[q, j * BLOCK:(j + 1) * BLOCK, :],
                (((1,), (1,)), ((), ())), preferred_element_type=jnp.float32)
        pltpu.make_async_copy(s_buf.at[q], s_out.at[q], os.at[q]).start()

    @pl.loop(0, CHUNKS + 2)
    def _(t):
        @pl.when(t < CHUNKS)
        def _():
            sort(t)

        @pl.when(t == 0)
        def _():
            forward(metas)

        @pl.when((t >= 1) & (t <= CHUNKS))
        def _():
            forward(chunk_copies(t - 1))

        @pl.when(t == 2)
        def _():
            prepare()

        @pl.when(t >= 2)
        def _():
            consume(t - 2)

    k_out[...] = acc[...].astype(jnp.bfloat16)

    @pl.loop(1, N_MEM)
    def _(o):
        meta_copy(o, mem).wait_send()

    def drain(copies):
        first, direct, _, again = copies
        for copy in first + direct + again:
            copy.wait_send()

    drain(metas)

    @pl.loop(0, CHUNKS)
    def _(q):
        @pl.loop(1, N_MEM)
        def _(o):
            image_copy(q, o, mem).wait_send()
        drain(chunk_copies(q))
        pltpu.make_async_copy(s_buf.at[q], s_out.at[q], os.at[q]).wait()


def exchange(images, meta, projections, weight, spread):
    vmem = pl.BlockSpec(memory_space=pltpu.VMEM)
    hbm = pl.BlockSpec(memory_space=pl.ANY)
    bf, f32 = jnp.bfloat16, jnp.float32
    dma = pltpu.SemaphoreType.DMA
    return pl.pallas_call(
        exchange_kernel,
        out_shape=(jax.ShapeDtypeStruct((CHUNKS, ROWS, W), bf), jax.ShapeDtypeStruct((len(PAIRS), BLOCK, BLOCK), bf)),
        in_specs=[hbm, vmem, hbm, vmem, vmem],
        out_specs=(hbm, vmem),
        scratch_shapes=[
            pltpu.VMEM((CHUNKS, COLS, W), bf),
            pltpu.VMEM((COLS, 128), bf),
            pltpu.VMEM((SLOTS, COLS), bf),
            pltpu.VMEM((CHUNKS, SLOTS, W), bf),
            pltpu.VMEM((CHUNKS, SLOTS, W), bf),
            pltpu.VMEM((CHUNKS, 2, PART, W), bf),
            pltpu.VMEM((SLOTS, 128), bf),
            pltpu.VMEM((SLOTS, 128), bf),
            pltpu.VMEM((2, PART, 128), bf),
            pltpu.VMEM((8, WIDTH), bf),
            pltpu.VMEM((ROWS, SLOTS), bf),
            pltpu.VMEM((SLOTS, 128), f32),
            pltpu.VMEM((SLOTS, 128), bf),
            pltpu.VMEM((CHUNKS, 8, W), f32),
            pltpu.VMEM((SLOTS, W), bf),
            pltpu.VMEM((CHUNKS, ROWS, W), bf),
            pltpu.VMEM((len(PAIRS), BLOCK, BLOCK), f32),
            dma((CHUNKS, N_MEM)), dma((CHUNKS, N_MEM)), dma((N_MEM,)), dma((N_MEM,)),
            dma((CHUNKS + 1, 8)), dma((CHUNKS + 1, 8)), dma((1,)), dma((CHUNKS + 1, 2)), dma((CHUNKS + 1, 2)),
            dma, dma((CHUNKS,)),
        ],
        compiler_params=pltpu.CompilerParams(collective_id=0, has_side_effects=True, vmem_limit_bytes=60 * 1024 * 1024),
        name="exchange",
    )(images, meta, projections, weight, spread)


def bmm(a, b):
    return jnp.einsum("nij,njk->nik", a, b, precision=HI)


def coefficients(gram, pixels):
    total = jnp.trace(gram, axis1=1, axis2=2)[:, None, None] + 1e-06
    scaled = gram / total
    ident = jnp.eye(gram.shape[1], dtype=jnp.float32)[None]
    first = 1.5 * ident - 0.5 * scaled
    later = bmm(bmm(first, scaled), first)
    second = 1.5 * ident - 0.5 * later
    return bmm(second, first) * jnp.sqrt(pixels / total)


def tree(gram, n_mem, rank, pixels):
    blocks = n_mem
    k = gram.reshape(n_mem, rank, n_mem, rank)
    chain = None
    while True:
        diag = jnp.stack([k[i, :, i, :] for i in range(blocks)])
        c = coefficients(diag, pixels)
        if chain is None:
            chain = c[:, :, None, :]
        else:
            chain = jnp.einsum("nij,njmk->nimk", c, chain, precision=HI)
        if blocks == 1:
            return chain.reshape(rank, n_mem * rank)
        k = jnp.einsum("aij,ajbk->aibk", c, k, precision=HI)
        k = jnp.einsum("aibk,blk->aibl", k, c, precision=HI)
        half = blocks // 2
        k = k.reshape(half, 2, rank, half, 2, rank).sum(axis=(1, 4))
        chain = chain.reshape(half, 2, rank, -1, rank).transpose(0, 2, 1, 3, 4).reshape(half, rank, -1, rank)
        blocks = half


def spread_matrix():
    column = np.arange(SLOTS)
    slot = column // PART * CAP + column % CAP
    return (np.arange(N_CLS * CAP)[:, None] == slot[None, :]).astype(np.float32)


def body(images, owner_group, bin_in_group, defocus, projections, sketch_weight):
    owners = owner_group[:, 0]
    onehot = (owners[:, None] == jnp.arange(N_CLS, dtype=jnp.int32)[None, :]).astype(jnp.int32)
    before = jnp.cumsum(onehot, axis=0) - onehot
    rank = jnp.sum(onehot * before, axis=1)
    target = owners * CAP + rank + 1
    lane = jnp.arange(128, dtype=jnp.int32)[None, :]
    meta = jnp.where(lane == 0, defocus.astype(jnp.float32)[:, None], 0.0)
    meta = jnp.where(lane == 1, bin_in_group.astype(jnp.float32)[:, None], meta)
    meta = jnp.where(lane == 2, 1.0, meta)
    meta = jnp.where(lane == 3, target.astype(jnp.float32)[:, None], meta).astype(jnp.bfloat16)
    spread = jnp.asarray(spread_matrix(), dtype=jnp.bfloat16)
    sketch, packed = exchange(images, meta, projections, sketch_weight, spread)
    packed = lax.psum(packed.astype(jnp.float32), "mem")
    n = ROWS // BLOCK
    blocks = [[None] * n for _ in range(n)]
    for at, (i, j) in enumerate(PAIRS):
        blocks[i][j] = packed[at]
        if i != j:
            blocks[j][i] = packed[at].T
    gram = jnp.concatenate([jnp.concatenate(r, axis=1) for r in blocks], axis=0)
    coef = tree(gram, N_MEM, RANK, float(PIX)).astype(jnp.bfloat16)
    result = jnp.einsum("km,qmw->kqw", coef, sketch, preferred_element_type=jnp.float32).astype(jnp.bfloat16)
    return result.reshape(1, RANK, WIDTH)


def solution(mesh):
    in_specs = (
        P(("cls", "mem"), None),
        P(("cls", "mem"), None),
        P(("cls", "mem")),
        P(("cls", "mem")),
        P("cls", None),
        P(),
    )
    out_specs = P("cls", None, "mem")
    return jax.shard_map(body, mesh=mesh, in_specs=in_specs, out_specs=out_specs, check_vma=False)
```

```python
import functools
import math

import jax
import jax.numpy as jnp
import numpy as np
from jax import lax
from jax.experimental import pallas as pl
from jax.experimental.pallas import tpu as pltpu
from jax.sharding import PartitionSpec as P

SIDE = 256
CAP = 6
N_CLS = 8
N_MEM = 16
RANK = 64
P_DEV = 24
P_PAD = 32
PIX = 65536
WIDTH = PIX // N_MEM
CHUNKS = 8
W = WIDTH // CHUNKS
PART = N_MEM * CAP
SLOTS = N_CLS * PART
ROWS = N_MEM * RANK
COLS = N_MEM * P_PAD
BLOCK = 256
PAIRS = [(i, j) for i in range(ROWS // BLOCK) for j in range(i, ROWS // BLOCK)]


def sine_terms():
    nodes = np.cos(np.pi * (np.arange(400) + 0.5) / 400) * 0.5
    basis = np.stack([nodes ** (2 * i + 1) for i in range(6)], axis=1)
    wanted = -math.sqrt(1.01) * np.sin(2 * np.pi * nodes)
    return [float(v) for v in np.linalg.lstsq(basis, wanted, rcond=None)[0]]


SINE = sine_terms()


def exchange_kernel(images, meta, proj, weight, spread, s_out, k_out, x_buf, m_buf, sel, send, recv, relay, smeta, rmeta, lmeta,
                    pj, wt, focus, table, grid_q, res, s_buf, acc,
                    xs, xr, ms, mr, ys, yr, fs, ls, lr, pm, os):
    cls = lax.axis_index("cls")
    mem = lax.axis_index("mem")
    y, core = cls // 2, cls % 2
    up, down, far = (y + 1) % 4, (y + 3) % 4, (y + 2) % 4
    z, x = mem // 4, mem % 4

    barrier = pltpu.get_barrier_semaphore()

    def peer(o):
        return ((z + o // 4) % 4) * 4 + (x + o % 4) % 4

    x_buf[...] = jnp.zeros_like(x_buf)
    m_buf[...] = jnp.zeros_like(m_buf)

    @pl.loop(1, N_MEM)
    def _(o):
        pl.semaphore_signal(barrier, inc=1, device_id={"mem": peer(o)}, device_id_type=pl.DeviceIdType.MESH)

    near = [up * 2, up * 2 + 1, down * 2, down * 2 + 1, y * 2 + 1 - core]
    for other in near:
        pl.semaphore_signal(barrier, inc=1, device_id={"cls": other}, device_id_type=pl.DeviceIdType.MESH)

    pl.semaphore_wait(barrier, N_MEM - 1 + len(near))

    def rows_of(ref, member):
        return ref.at[pl.ds(pl.multiple_of(member * P_PAD, P_PAD), P_DEV), :]

    def meta_copy(o, owner):
        return pltpu.make_async_remote_copy(
            src_ref=meta, dst_ref=rows_of(m_buf, owner), send_sem=ms.at[o], recv_sem=mr.at[owner],
            device_id={"mem": peer(o)}, device_id_type=pl.DeviceIdType.MESH)

    def image_part(q, target):
        return images.at[:, pl.ds(pl.multiple_of(target * WIDTH + q * W, W), W)]

    def image_copy(q, o, owner):
        return pltpu.make_async_remote_copy(
            src_ref=image_part(q, peer(o)), dst_ref=rows_of(x_buf.at[q], owner),
            send_sem=xs.at[q, o], recv_sem=xr.at[q, owner],
            device_id={"mem": peer(o)}, device_id_type=pl.DeviceIdType.MESH)

    def own_image(q):
        return pltpu.make_async_copy(image_part(q, mem), rows_of(x_buf.at[q], mem), xs.at[q, 0])

    own_meta = pltpu.make_async_copy(meta, rows_of(m_buf, mem), ms.at[0])
    own_meta.start()

    @pl.loop(1, N_MEM)
    def _(o):
        meta_copy(o, mem).start()

    @pl.loop(0, CHUNKS)
    def _(q):
        own_image(q).start()

        @pl.loop(1, N_MEM)
        def _(o):
            image_copy(q, o, mem).start()

    own_proj = pltpu.make_async_copy(proj.at[:, pl.ds(pl.multiple_of(mem * WIDTH, WIDTH), WIDTH)], pj, pm)
    own_proj.start()

    wide = jnp.dot(weight[...], spread[...], preferred_element_type=jnp.float32)
    column = lax.broadcasted_iota(jnp.int32, (RANK, SLOTS), 1).astype(jnp.float32)
    local = column - PART * jnp.floor((column + 0.5) * (1.0 / PART))
    holder = jnp.floor((local + 0.5) * (1.0 / CAP))
    for m in range(N_MEM):
        wt[m * RANK:(m + 1) * RANK, :] = jnp.where(holder == float(m), wide, 0.0).astype(jnp.bfloat16)

    @pl.loop(0, CHUNKS)
    def _(q):
        place = mem * WIDTH + q * W + lax.broadcasted_iota(jnp.int32, (8, W), 1)
        col = place & (SIDE - 1)
        row = lax.shift_right_logical(place, 8)
        fx = jnp.where(col < SIDE // 2, col, col - SIDE).astype(jnp.float32) * (1.0 / SIDE)
        fy = jnp.where(row < SIDE // 2, row, row - SIDE).astype(jnp.float32) * (1.0 / SIDE)
        grid_q[q] = (fx * fx + fy * fy) * (160.0 / (2 * math.pi))

    acc[...] = jnp.zeros_like(acc)

    own_meta.wait()

    @pl.loop(1, N_MEM)
    def _(o):
        owner = peer(N_MEM - o)
        meta_copy(o, peer(o)).wait_recv()

    lane = lax.broadcasted_iota(jnp.int32, (8, 128), 1)
    third = jnp.where(lane == 3, 1.0, 0.0).astype(jnp.bfloat16)
    code = lax.dot_general(third, m_buf[...], (((1,), (1,)), ((), ())), preferred_element_type=jnp.float32)
    which = lax.shift_right_logical(lax.broadcasted_iota(jnp.int32, (1, COLS), 1), 5).astype(jnp.float32)
    code = code[0:1, :] + 64.0 * which
    item = lax.broadcasted_iota(jnp.int32, (PART, COLS), 0).astype(jnp.float32)
    whose = jnp.floor((item + 0.5) * (1.0 / CAP))
    base = whose * 64.0 + (item - CAP * whose) + 1.0 - code
    for c in range(N_CLS):
        sel[c * PART:(c + 1) * PART, :] = jnp.where(base == -float(c * CAP), 1.0, 0.0).astype(jnp.bfloat16)

    def part_of(ref, group):
        return ref.at[pl.ds(pl.multiple_of(group * PART, PART), PART), :]

    def y_copies(src, dst, mid, sems, rsems, msems, mrsems):
        def remote(a, b, s, r, target):
            return pltpu.make_async_remote_copy(src_ref=a, dst_ref=b, send_sem=s, recv_sem=r,
                                                device_id={"cls": target}, device_id_type=pl.DeviceIdType.MESH)
        here = part_of(dst, cls)
        first = [
            remote(part_of(src, far * 2), mid.at[0], msems.at[0], mrsems.at[0], up * 2 + core),
            remote(part_of(src, far * 2 + 1), mid.at[1], msems.at[1], mrsems.at[1], down * 2 + core),
        ]
        direct = [remote(part_of(src, other), here, sems.at[i], rsems.at[cls], other) for i, other in enumerate(near)]
        own = pltpu.make_async_copy(part_of(src, cls), here, rsems.at[cls])
        again = [
            remote(mid.at[0], part_of(dst, down * 2 + core), sems.at[5], rsems.at[down * 2 + core], up * 2),
            remote(mid.at[1], part_of(dst, up * 2 + core), sems.at[6], rsems.at[up * 2 + core], down * 2 + 1),
        ]
        return first, direct, own, again

    def arrivals(dst, sems, rsems):
        def wait(source):
            pltpu.make_async_remote_copy(
                src_ref=part_of(dst, source), dst_ref=part_of(dst, source), send_sem=sems.at[0], recv_sem=rsems.at[source],
                device_id={"cls": up * 2}, device_id_type=pl.DeviceIdType.MESH).wait_recv()
        for other in near + [far * 2, far * 2 + 1]:
            wait(other)

    metas = y_copies(smeta, rmeta, lmeta, ys.at[CHUNKS], yr.at[CHUNKS], ls.at[CHUNKS], lr.at[CHUNKS])
    smeta[...] = jnp.dot(sel[...], m_buf[...], preferred_element_type=jnp.float32).astype(jnp.bfloat16)
    for copy in metas[0] + metas[1] + [metas[2]]:
        copy.start()

    def chunk_copies(q):
        return y_copies(send.at[q], recv.at[q], relay.at[q], ys.at[q], yr.at[q], ls.at[q], lr.at[q])

    def sort(q):
        own_image(q).wait()

        @pl.loop(1, N_MEM)
        def _(o):
            image_copy(q, o, peer(o)).wait_recv()

        send[q] = jnp.dot(sel[...], x_buf[q], preferred_element_type=jnp.float32).astype(jnp.bfloat16)
        first, direct, own, _ = chunk_copies(q)
        for copy in first + direct + [own]:
            copy.start()

    def forward(copies):
        first, _, _, again = copies
        for a, b in zip(first, again):
            a.wait_recv()
            b.start()

    def prepare():
        metas[2].wait()
        arrivals(rmeta, ys.at[CHUNKS], yr.at[CHUNKS])
        pick = lax.broadcasted_iota(jnp.int32, (128, 128), 0)
        m = rmeta[...]
        def lanes(i):
            return jnp.dot(m, jnp.where(pick == i, 1.0, 0.0).astype(jnp.bfloat16), preferred_element_type=jnp.float32)
        focus[...] = lanes(0)
        at = lax.broadcasted_iota(jnp.int32, (SLOTS, 128), 1).astype(jnp.float32)
        table[...] = jnp.where((lanes(1) == at) & (lanes(2) == 1.0), 1.0, 0.0).astype(jnp.bfloat16)
        own_proj.wait()

    def consume(q):
        _, _, own, _ = chunk_copies(q)
        own.wait()
        arrivals(recv.at[q], ys.at[q], yr.at[q])
        projected = pj[:, pl.ds(pl.multiple_of(q * W, W), W)]

        @pl.loop(0, SLOTS // 16)
        def _(i):
            r = pl.ds(pl.multiple_of(i * 16, 16), 16)
            chosen = jnp.dot(table[r, 0:8], projected, preferred_element_type=jnp.float32)
            f = focus[r, :]
            for l in range(W // 128):
                cols = slice(l * 128, (l + 1) * 128)
                g = grid_q[q, :, cols]
                turn = f * jnp.concatenate([g, g], axis=0) + math.atan(0.1) / (2 * math.pi)
                turn = turn - jnp.round(turn)
                sq = turn * turn
                value = SINE[5]
                for term in SINE[4::-1]:
                    value = value * sq + term
                ctf = value * turn
                got = recv[q, r, cols].astype(jnp.float32)
                res[r, cols] = (got - ctf * chosen[:, cols]).astype(jnp.bfloat16)

        s_buf[q] = jnp.dot(wt[...], res[...], preferred_element_type=jnp.float32).astype(jnp.bfloat16)
        for n, (i, j) in enumerate(PAIRS):
            acc[n] += lax.dot_general(
                s_buf[q, i * BLOCK:(i + 1) * BLOCK, :], s_buf[q, j * BLOCK:(j + 1) * BLOCK, :],
                (((1,), (1,)), ((), ())), preferred_element_type=jnp.float32)
        pltpu.make_async_copy(s_buf.at[q], s_out.at[q], os.at[q]).start()

    @pl.loop(0, CHUNKS + 2)
    def _(t):
        @pl.when(t < CHUNKS)
        def _():
            sort(t)

        @pl.when(t == 0)
        def _():
            forward(metas)

        @pl.when((t >= 1) & (t <= CHUNKS))
        def _():
            forward(chunk_copies(t - 1))

        @pl.when(t == 2)
        def _():
            prepare()

        @pl.when(t >= 2)
        def _():
            consume(t - 2)

    k_out[...] = acc[...].astype(jnp.bfloat16)

    @pl.loop(1, N_MEM)
    def _(o):
        meta_copy(o, mem).wait_send()

    def drain(copies):
        first, direct, _, again = copies
        for copy in first + direct + again:
            copy.wait_send()

    drain(metas)

    @pl.loop(0, CHUNKS)
    def _(q):
        @pl.loop(1, N_MEM)
        def _(o):
            image_copy(q, o, mem).wait_send()
        drain(chunk_copies(q))
        pltpu.make_async_copy(s_buf.at[q], s_out.at[q], os.at[q]).wait()


def exchange(images, meta, projections, weight, spread):
    vmem = pl.BlockSpec(memory_space=pltpu.VMEM)
    hbm = pl.BlockSpec(memory_space=pl.ANY)
    bf, f32 = jnp.bfloat16, jnp.float32
    dma = pltpu.SemaphoreType.DMA
    return pl.pallas_call(
        exchange_kernel,
        out_shape=(jax.ShapeDtypeStruct((CHUNKS, ROWS, W), bf), jax.ShapeDtypeStruct((len(PAIRS), BLOCK, BLOCK), bf)),
        in_specs=[hbm, vmem, hbm, vmem, vmem],
        out_specs=(hbm, vmem),
        scratch_shapes=[
            pltpu.VMEM((CHUNKS, COLS, W), bf),
            pltpu.VMEM((COLS, 128), bf),
            pltpu.VMEM((SLOTS, COLS), bf),
            pltpu.VMEM((CHUNKS, SLOTS, W), bf),
            pltpu.VMEM((CHUNKS, SLOTS, W), bf),
            pltpu.VMEM((CHUNKS, 2, PART, W), bf),
            pltpu.VMEM((SLOTS, 128), bf),
            pltpu.VMEM((SLOTS, 128), bf),
            pltpu.VMEM((2, PART, 128), bf),
            pltpu.VMEM((8, WIDTH), bf),
            pltpu.VMEM((ROWS, SLOTS), bf),
            pltpu.VMEM((SLOTS, 128), f32),
            pltpu.VMEM((SLOTS, 128), bf),
            pltpu.VMEM((CHUNKS, 8, W), f32),
            pltpu.VMEM((SLOTS, W), bf),
            pltpu.VMEM((CHUNKS, ROWS, W), bf),
            pltpu.VMEM((len(PAIRS), BLOCK, BLOCK), f32),
            dma((CHUNKS, N_MEM)), dma((CHUNKS, N_MEM)), dma((N_MEM,)), dma((N_MEM,)),
            dma((CHUNKS + 1, 8)), dma((CHUNKS + 1, 8)), dma((1,)), dma((CHUNKS + 1, 2)), dma((CHUNKS + 1, 2)),
            dma, dma((CHUNKS,)),
        ],
        compiler_params=pltpu.CompilerParams(collective_id=0, has_side_effects=True, vmem_limit_bytes=60 * 1024 * 1024),
        name="exchange",
    )(images, meta, projections, weight, spread)


def narrow(value):
    return value.astype(jnp.bfloat16)


def dot(a, b):
    return jnp.dot(narrow(a), narrow(b), preferred_element_type=jnp.float32)


def dot_t(a, b):
    return lax.dot_general(narrow(a), narrow(b), (((1,), (1,)), ((), ())), preferred_element_type=jnp.float32)


def normalise(gram):
    n = gram.shape[0]
    row = lax.broadcasted_iota(jnp.int32, (n, n), 0)
    col = lax.broadcasted_iota(jnp.int32, (n, n), 1)
    diag = jnp.sum(jnp.where(row == col, gram, 0.0), axis=0, keepdims=True)
    same = lax.shift_right_logical(row, 6) == lax.shift_right_logical(col, 6)
    total = jnp.sum(jnp.where(same, diag, 0.0), axis=1, keepdims=True) + 1e-06
    g = jnp.where(same, gram, 0.0) / total
    g2 = dot(g, g)
    rest = -2.4375 * g + 1.6875 * g2 + dot(g2, -0.5625 * g + 0.0625 * g2)
    return rest, jnp.sqrt(float(PIX) / total)


def advance(gram, factor):
    rest, scale = normalise(gram)
    return scale * (2.25 * factor + dot(rest, factor))


def merged_factors(block):
    quads = ROWS // BLOCK
    row = lax.broadcasted_iota(jnp.int32, (BLOCK, BLOCK), 0)
    col = lax.broadcasted_iota(jnp.int32, (BLOCK, BLOCK), 1)
    ident = jnp.where(row == col, 1.0, 0.0)
    chain = []
    for q in range(quads):
        rest, scale = normalise(block(q, q).astype(jnp.float32))
        chain.append(scale * (2.25 * ident + rest))
    for level in range(2):
        step = RANK << level
        for q in range(quads):
            d = chain[q]
            swapped = jnp.concatenate([d[a ^ step:(a ^ step) + step] for a in range(0, BLOCK, step)], axis=0)
            joined = d + swapped
            chain[q] = advance(dot_t(dot(joined, block(q, q)), joined), joined)
    chain = [d[:RANK] for d in chain]
    size = 2
    while size <= quads:
        for first in range(0, quads, size):
            group = range(first, first + size)
            gram = None
            for j in group:
                t = None
                for i in group:
                    part = dot(chain[i], block(i, j)) if i <= j else dot_t(chain[i], block(j, i))
                    t = part if t is None else t + part
                part = dot_t(t, chain[j])
                gram = part if gram is None else gram + part
            rest, scale = normalise(gram)
            for i in group:
                chain[i] = scale * (2.25 * chain[i] + dot(rest, chain[i]))
        size *= 2
    return chain


EIGHTH = len(PAIRS) * BLOCK // 2
FOURTH = EIGHTH // 4
LAST = FOURTH // 4


def merge_kernel(packed, s_in, out, first_in, mid, second_in, gath, s_buf, coef, s1, r1, s2, r2, s3, r3, s4, r4, ss):
    mem = lax.axis_index("mem")
    z, x = mem // 4, mem % 4
    barrier = pltpu.get_barrier_semaphore()

    def along_x(d):
        return z * 4 + (x + d) % 4

    def along_z(d):
        return ((z + d) % 4) * 4 + x

    for d in range(1, 4):
        for target in (along_x(d), along_z(d)):
            pl.semaphore_signal(barrier, inc=1, device_id={"mem": target}, device_id_type=pl.DeviceIdType.MESH)
    for q in range(CHUNKS):
        pltpu.make_async_copy(s_in.at[q], s_buf.at[q], ss.at[q]).start()
    pl.semaphore_wait(barrier, 6)

    axes = [(x, z, along_x, along_z), (z, x, along_z, along_x)]

    def rows(ref, start, size):
        return ref.at[pl.ds(pl.multiple_of(start, 16), size), :]

    def remote(src, dst, s, r, target):
        return pltpu.make_async_remote_copy(src_ref=src, dst_ref=dst, send_sem=s, recv_sem=r,
                                            device_id={"mem": target}, device_id_type=pl.DeviceIdType.MESH)

    def stage_1(h, d):
        a, b, one, two = axes[h]
        return remote(rows(packed, h * EIGHTH + (a + d) % 4 * FOURTH, FOURTH), first_in.at[h, d - 1],
                      s1.at[h, d - 1], r1.at[h, d - 1], one(d))

    def stage_2(h, d):
        a, b, one, two = axes[h]
        return remote(rows(mid.at[h], (b + d) % 4 * LAST, LAST), second_in.at[h, d - 1],
                      s2.at[h, d - 1], r2.at[h, d - 1], two(d))

    def stage_3(h, d, back=0):
        a, b, one, two = axes[h]
        here = rows(gath, h * EIGHTH + a * FOURTH + (b + back) % 4 * LAST, LAST)
        return remote(here, here, s3.at[h, d - 1], r3.at[h, d - 1], two(d))

    def stage_4(h, d, back=0):
        a, b, one, two = axes[h]
        here = rows(gath, h * EIGHTH + (a + back) % 4 * FOURTH, FOURTH)
        return remote(here, here, s4.at[h, d - 1], r4.at[h, d - 1], one(d))

    def value(ref):
        return ref[...].astype(jnp.float32)

    for d in (2, 1, 3):
        for h in range(2):
            stage_1(h, d).start()
    for h in range(2):
        a, b, one, two = axes[h]
        for d in range(1, 4):
            stage_1(h, d).wait_recv()
        mid[h] = narrow(value(rows(packed, h * EIGHTH + a * FOURTH, FOURTH))
                        + value(first_in.at[h, 0]) + value(first_in.at[h, 1]) + value(first_in.at[h, 2]))
        for d in (2, 1, 3):
            stage_2(h, d).start()
    for h in range(2):
        a, b, one, two = axes[h]
        for d in range(1, 4):
            stage_2(h, d).wait_recv()
        start = pl.multiple_of(h * EIGHTH + a * FOURTH + b * LAST, 16)
        gath[pl.ds(start, LAST), :] = narrow(value(rows(mid.at[h], b * LAST, LAST))
                                             + value(second_in.at[h, 0]) + value(second_in.at[h, 1]) + value(second_in.at[h, 2]))
        for d in (2, 1, 3):
            stage_3(h, d).start()
    for h in range(2):
        for d in range(1, 4):
            stage_3(h, d, -d + 4).wait_recv()
        for d in (2, 1, 3):
            stage_4(h, d).start()
    for h in range(2):
        for d in range(1, 4):
            stage_4(h, d, -d + 4).wait_recv()

    def block(i, j):
        n = PAIRS.index((i, j))
        return gath[n * BLOCK:(n + 1) * BLOCK, :]

    for q, factor in enumerate(merged_factors(block)):
        coef[:, q * BLOCK:(q + 1) * BLOCK] = narrow(factor)

    for q in range(CHUNKS):
        pltpu.make_async_copy(s_in.at[q], s_buf.at[q], ss.at[q]).wait()
        out[:, q * W:(q + 1) * W] = narrow(jnp.dot(coef[...], s_buf[q], preferred_element_type=jnp.float32))

    for h in range(2):
        for d in range(1, 4):
            for stage in (stage_1, stage_2, stage_3, stage_4):
                stage(h, d).wait_send()


def merge(packed, sketch):
    vmem = pl.BlockSpec(memory_space=pltpu.VMEM)
    hbm = pl.BlockSpec(memory_space=pl.ANY)
    bf = jnp.bfloat16
    dma = pltpu.SemaphoreType.DMA
    return pl.pallas_call(
        merge_kernel,
        out_shape=jax.ShapeDtypeStruct((RANK, WIDTH), bf),
        in_specs=[vmem, hbm],
        out_specs=vmem,
        scratch_shapes=[
            pltpu.VMEM((2, 3, FOURTH, BLOCK), bf),
            pltpu.VMEM((2, FOURTH, BLOCK), bf),
            pltpu.VMEM((2, 3, LAST, BLOCK), bf),
            pltpu.VMEM((2 * EIGHTH, BLOCK), bf),
            pltpu.VMEM((CHUNKS, ROWS, W), bf),
            pltpu.VMEM((RANK, ROWS), bf),
        ] + [dma((2, 3))] * 8 + [dma((CHUNKS,))],
        compiler_params=pltpu.CompilerParams(collective_id=1, has_side_effects=True, vmem_limit_bytes=60 * 1024 * 1024),
        name="merge",
    )(packed.reshape(2 * EIGHTH, BLOCK), sketch)


def spread_matrix():
    column = np.arange(SLOTS)
    slot = column // PART * CAP + column % CAP
    return (np.arange(N_CLS * CAP)[:, None] == slot[None, :]).astype(np.float32)


def body(images, owner_group, bin_in_group, defocus, projections, sketch_weight):
    owners = owner_group[:, 0]
    onehot = (owners[:, None] == jnp.arange(N_CLS, dtype=jnp.int32)[None, :]).astype(jnp.int32)
    before = jnp.cumsum(onehot, axis=0) - onehot
    rank = jnp.sum(onehot * before, axis=1)
    target = owners * CAP + rank + 1
    lane = jnp.arange(128, dtype=jnp.int32)[None, :]
    meta = jnp.where(lane == 0, defocus.astype(jnp.float32)[:, None], 0.0)
    meta = jnp.where(lane == 1, bin_in_group.astype(jnp.float32)[:, None], meta)
    meta = jnp.where(lane == 2, 1.0, meta)
    meta = jnp.where(lane == 3, target.astype(jnp.float32)[:, None], meta).astype(jnp.bfloat16)
    spread = jnp.asarray(spread_matrix(), dtype=jnp.bfloat16)
    sketch, packed = exchange(images, meta, projections, sketch_weight, spread)
    return merge(packed, sketch)[None]


def solution(mesh):
    in_specs = (
        P(("cls", "mem"), None),
        P(("cls", "mem"), None),
        P(("cls", "mem")),
        P(("cls", "mem")),
        P("cls", None),
        P(),
    )
    out_specs = P("cls", None, "mem")
    return jax.shard_map(body, mesh=mesh, in_specs=in_specs, out_specs=out_specs, check_vma=False)
```

```python
import functools
import math

import jax
import jax.numpy as jnp
import numpy as np
from jax import lax
from jax.experimental import pallas as pl
from jax.experimental.pallas import tpu as pltpu
from jax.sharding import PartitionSpec as P

SIDE = 256
CAP = 6
N_CLS = 8
N_MEM = 16
RANK = 64
P_DEV = 24
P_PAD = 32
PIX = 65536
WIDTH = PIX // N_MEM
CHUNKS = 8
W = WIDTH // CHUNKS
PART = N_MEM * CAP
SLOTS = N_CLS * PART
ROWS = N_MEM * RANK
COLS = N_MEM * P_PAD
BLOCK = 256
PAIRS = [(i, j) for i in range(SLOTS // BLOCK) for j in range(i, SLOTS // BLOCK)]
QUADS = ROWS // BLOCK
QUAD_PAIRS = [(i, j) for i in range(QUADS) for j in range(i, QUADS)]
HALF = len(PAIRS) * BLOCK // 2
FOURTH = HALF // 4
LAST = FOURTH // 4
MESH = pl.DeviceIdType.MESH


def sine_terms():
    nodes = np.cos(np.pi * (np.arange(400) + 0.5) / 400) * 0.5
    basis = np.stack([nodes ** (2 * i + 1) for i in range(6)], axis=1)
    wanted = -math.sqrt(1.01) * np.sin(2 * np.pi * nodes)
    return [float(v) for v in np.linalg.lstsq(basis, wanted, rcond=None)[0]]


SINE = sine_terms()
ROUND = 12582912.0
STRIP = 16


def narrow(value):
    return value.astype(jnp.bfloat16)


def dot(a, b):
    return jnp.dot(narrow(a), narrow(b), preferred_element_type=jnp.float32)


def dot_t(a, b):
    return lax.dot_general(narrow(a), narrow(b), (((1,), (1,)), ((), ())), preferred_element_type=jnp.float32)


def normalise(gram):
    n = gram.shape[0]
    row = lax.broadcasted_iota(jnp.int32, (n, n), 0)
    col = lax.broadcasted_iota(jnp.int32, (n, n), 1)
    diag = jnp.sum(jnp.where(row == col, gram, 0.0), axis=0, keepdims=True)
    same = lax.shift_right_logical(row, 6) == lax.shift_right_logical(col, 6)
    total = jnp.sum(jnp.where(same, diag, 0.0), axis=1, keepdims=True) + 1e-06
    g = jnp.where(same, gram, 0.0) / total
    g2 = dot(g, g)
    rest = -2.4375 * g + 1.6875 * g2 + dot(g2, -0.5625 * g + 0.0625 * g2)
    return rest, jnp.sqrt(float(PIX) / total)


def advance(gram, factor):
    rest, scale = normalise(gram)
    return scale * (2.25 * factor + dot(rest, factor))


def merged_factors(block):
    row = lax.broadcasted_iota(jnp.int32, (BLOCK, BLOCK), 0)
    col = lax.broadcasted_iota(jnp.int32, (BLOCK, BLOCK), 1)
    ident = jnp.where(row == col, 1.0, 0.0)
    chain = []
    for q in range(QUADS):
        rest, scale = normalise(block(q, q).astype(jnp.float32))
        chain.append(scale * (2.25 * ident + rest))
    for level in range(2):
        step = RANK << level
        for q in range(QUADS):
            d = chain[q]
            swapped = jnp.concatenate([d[a ^ step:(a ^ step) + step] for a in range(0, BLOCK, step)], axis=0)
            joined = d + swapped
            chain[q] = advance(dot_t(dot(joined, block(q, q)), joined), joined)
    chain = [d[:RANK] for d in chain]
    size = 2
    while size <= QUADS:
        for first in range(0, QUADS, size):
            group = range(first, first + size)
            gram = None
            for j in group:
                t = None
                for i in group:
                    part = dot(chain[i], block(i, j)) if i <= j else dot_t(chain[i], block(j, i))
                    t = part if t is None else t + part
                part = dot_t(t, chain[j])
                gram = part if gram is None else gram + part
            rest, scale = normalise(gram)
            for i in group:
                chain[i] = scale * (2.25 * chain[i] + dot(rest, chain[i]))
        size *= 2
    return chain


def kernel(images, owner, bins, defocus, proj, weight, spread, out, x_buf, m_own, m_buf, sel, send, recv, smeta, rmeta,
           pj, wt, focus, table, grid_q, chosen, res, acc, packed, first_in, mid, second_in, gath, turned, gram, coef,
           xs, xr, ms, mr, ys, yr, pm, s1, r1, s2, r2, s3, r3, s4, r4):
    cls = lax.axis_index("cls")
    mem = lax.axis_index("mem")
    y, core = cls // 2, cls % 2
    up, down, far = (y + 1) % 4, (y + 3) % 4, (y + 2) % 4
    z, x = mem // 4, mem % 4

    barrier = pltpu.get_barrier_semaphore()

    def peer(o):
        return ((z + o // 4) % 4) * 4 + (x + o % 4) % 4

    x_buf[...] = jnp.zeros_like(x_buf)
    m_buf[...] = jnp.zeros_like(m_buf)

    @pl.loop(1, N_MEM)
    def _(o):
        pl.semaphore_signal(barrier, inc=1, device_id={"mem": peer(o)}, device_id_type=MESH)

    others = [far * 2, far * 2 + 1, up * 2, down * 2 + 1, up * 2 + 1, down * 2, y * 2 + 1 - core]
    for other in others:
        pl.semaphore_signal(barrier, inc=1, device_id={"cls": other}, device_id_type=MESH)


    lane = lax.broadcasted_iota(jnp.int32, (P_DEV, 128), 1)
    row = lax.broadcasted_iota(jnp.int32, (P_DEV, P_DEV), 0)
    col = lax.broadcasted_iota(jnp.int32, (P_DEV, P_DEV), 1)
    def upright(values):
        return jnp.sum(jnp.where(row == col, values.astype(jnp.float32), 0.0), axis=1, keepdims=True)

    who = upright(owner[...])
    onehot = jnp.where(lane.astype(jnp.float32) == who, 1.0, 0.0)
    before = dot(jnp.where(col < row, 1.0, 0.0), onehot)
    rank = jnp.sum(onehot * before, axis=1, keepdims=True)
    meta = jnp.where(lane == 0, upright(defocus[...]), 0.0)
    meta = jnp.where(lane == 1, upright(bins[...]), meta)
    meta = jnp.where(lane == 2, 1.0, meta)
    m_own[...] = narrow(jnp.where(lane == 3, CAP * who + rank + 1.0, meta))
    pl.semaphore_wait(barrier, N_MEM - 1 + len(others))

    def rows_of(ref, member):
        return ref.at[pl.ds(pl.multiple_of(member * P_PAD, P_PAD), P_DEV), :]

    def meta_copy(o, owner):
        return pltpu.make_async_remote_copy(
            src_ref=m_own, dst_ref=rows_of(m_buf, owner), send_sem=ms.at[o], recv_sem=mr.at[owner],
            device_id={"mem": peer(o)}, device_id_type=MESH)

    def image_part(q, target):
        return images.at[:, pl.ds(pl.multiple_of(target * WIDTH + q * W, W), W)]

    def image_copy(q, o, owner):
        return pltpu.make_async_remote_copy(
            src_ref=image_part(q, peer(o)), dst_ref=rows_of(x_buf.at[q], owner),
            send_sem=xs.at[q, o], recv_sem=xr.at[q, owner],
            device_id={"mem": peer(o)}, device_id_type=MESH)

    def own_image(q):
        return pltpu.make_async_copy(image_part(q, mem), rows_of(x_buf.at[q], mem), xs.at[q, 0])

    own_meta = pltpu.make_async_copy(m_own, rows_of(m_buf, mem), ms.at[0])
    own_meta.start()

    @pl.loop(1, N_MEM)
    def _(o):
        meta_copy(o, mem).start()

    @pl.loop(0, CHUNKS)
    def _(q):
        own_image(q).start()

        @pl.loop(1, N_MEM)
        def _(o):
            image_copy(q, o, mem).start()

    own_proj = pltpu.make_async_copy(proj.at[:, pl.ds(pl.multiple_of(mem * WIDTH, WIDTH), WIDTH)], pj, pm)
    own_proj.start()

    wide = lax.dot_general(weight[...], spread[...], (((0,), (0,)), ((), ())), preferred_element_type=jnp.float32)
    column = lax.broadcasted_iota(jnp.int32, (RANK, SLOTS), 1).astype(jnp.float32)
    local = column - PART * jnp.floor((column + 0.5) * (1.0 / PART))
    holder = jnp.floor((local + 0.5) * (1.0 / CAP))
    for m in range(N_MEM):
        wt[m * RANK:(m + 1) * RANK, :] = jnp.where(holder == float(m), wide, 0.0).astype(jnp.bfloat16)

    @pl.loop(0, CHUNKS)
    def _(q):
        place = mem * WIDTH + q * W + lax.broadcasted_iota(jnp.int32, (8, W), 1)
        col = place & (SIDE - 1)
        row = lax.shift_right_logical(place, 8)
        fx = jnp.where(col < SIDE // 2, col, col - SIDE).astype(jnp.float32) * (1.0 / SIDE)
        fy = jnp.where(row < SIDE // 2, row, row - SIDE).astype(jnp.float32) * (1.0 / SIDE)
        grid_q[q] = (fx * fx + fy * fy) * (160.0 / (2 * math.pi))

    acc[...] = jnp.zeros_like(acc)

    own_meta.wait()

    @pl.loop(1, N_MEM)
    def _(o):
        owner = peer(N_MEM - o)
        meta_copy(o, peer(o)).wait_recv()

    lane = lax.broadcasted_iota(jnp.int32, (8, 128), 1)
    third = jnp.where(lane == 3, 1.0, 0.0).astype(jnp.bfloat16)
    code = lax.dot_general(third, m_buf[...], (((1,), (1,)), ((), ())), preferred_element_type=jnp.float32)
    which = lax.shift_right_logical(lax.broadcasted_iota(jnp.int32, (1, COLS), 1), 5).astype(jnp.float32)
    code = code[0:1, :] + 64.0 * which
    item = lax.broadcasted_iota(jnp.int32, (PART, COLS), 0).astype(jnp.float32)
    whose = jnp.floor((item + 0.5) * (1.0 / CAP))
    base = whose * 64.0 + (item - CAP * whose) + 1.0 - code
    for c in range(N_CLS):
        sel[c * PART:(c + 1) * PART, :] = jnp.where(base == -float(c * CAP), 1.0, 0.0).astype(jnp.bfloat16)

    def part_of(ref, group):
        return ref.at[pl.ds(pl.multiple_of(group * PART, PART), PART), :]

    def y_copies(src, dst, sems, rsems):
        here = part_of(dst, cls)
        return [pltpu.make_async_remote_copy(
            src_ref=part_of(src, other), dst_ref=here, send_sem=sems.at[i], recv_sem=rsems.at[cls],
            device_id={"cls": other}, device_id_type=MESH) for i, other in enumerate(others)]

    def y_own(src, dst, rsems):
        return pltpu.make_async_copy(part_of(src, cls), part_of(dst, cls), rsems.at[cls])

    def arrivals(dst, sems, rsems):
        for source in others:
            pltpu.make_async_remote_copy(
                src_ref=part_of(dst, source), dst_ref=part_of(dst, source), send_sem=sems.at[0], recv_sem=rsems.at[source],
                device_id={"cls": source}, device_id_type=MESH).wait_recv()

    last = CHUNKS
    smeta[...] = jnp.dot(sel[...], m_buf[...], preferred_element_type=jnp.float32).astype(jnp.bfloat16)
    for copy in y_copies(smeta, rmeta, ys.at[last], yr.at[last]):
        copy.start()
    y_own(smeta, rmeta, yr.at[last]).start()

    def sort(q):
        own_image(q).wait()

        @pl.loop(1, N_MEM)
        def _(o):
            image_copy(q, o, peer(o)).wait_recv()

        send[q] = jnp.dot(sel[...], x_buf[q], preferred_element_type=jnp.float32).astype(jnp.bfloat16)
        for copy in y_copies(send.at[q], recv.at[q], ys.at[q], yr.at[q]):
            copy.start()
        y_own(send.at[q], recv.at[q], yr.at[q]).start()

    def prepare():
        y_own(smeta, rmeta, yr.at[last]).wait()
        arrivals(rmeta, ys.at[last], yr.at[last])
        pick = lax.broadcasted_iota(jnp.int32, (128, 128), 0)
        m = rmeta[...]
        def lanes(i):
            return jnp.dot(m, jnp.where(pick == i, 1.0, 0.0).astype(jnp.bfloat16), preferred_element_type=jnp.float32)
        focus[...] = lanes(0)
        at = lax.broadcasted_iota(jnp.int32, (SLOTS, 128), 1).astype(jnp.float32)
        table[...] = jnp.where((lanes(1) == at) & (lanes(2) == 1.0), 1.0, 0.0).astype(jnp.bfloat16)
        own_proj.wait()

    def consume(q):
        y_own(send.at[q], recv.at[q], yr.at[q]).wait()
        arrivals(recv.at[q], ys.at[q], yr.at[q])
        projected = pj[:, pl.ds(pl.multiple_of(q * W, W), W)]
        chosen[...] = jnp.dot(table[:, 0:8], projected, preferred_element_type=jnp.float32).astype(jnp.bfloat16)

        @pl.loop(0, SLOTS // STRIP, unroll=2)
        def _(i):
            r = pl.ds(pl.multiple_of(i * STRIP, STRIP), STRIP)
            f = focus[r, :]
            for l in range(W // 128):
                cols = slice(l * 128, (l + 1) * 128)
                g = grid_q[q, :, cols]
                turn = f * jnp.concatenate([g] * (STRIP // 8), axis=0) + math.atan(0.1) / (2 * math.pi)
                turn = turn - ((turn + ROUND) - ROUND)
                sq = turn * turn
                value = SINE[5]
                for term in SINE[4::-1]:
                    value = value * sq + term
                ctf = value * turn
                got = recv[q, r, cols].astype(jnp.float32)
                res[q, r, cols] = (got - ctf * chosen[r, cols].astype(jnp.float32)).astype(jnp.bfloat16)

        for n, (i, j) in enumerate(PAIRS):
            acc[n] += dot_t(res[q, i * BLOCK:(i + 1) * BLOCK, :], res[q, j * BLOCK:(j + 1) * BLOCK, :])

    @pl.loop(0, CHUNKS + 2)
    def _(t):
        @pl.when(t < CHUNKS)
        def _():
            sort(t)

        @pl.when(t == 2)
        def _():
            prepare()

        @pl.when(t >= 2)
        def _():
            consume(t - 2)

    for n in range(len(PAIRS)):
        packed[n * BLOCK:(n + 1) * BLOCK, :] = narrow(acc[n])

    def along_x(d):
        return z * 4 + (x + d) % 4

    def along_z(d):
        return ((z + d) % 4) * 4 + x

    axes = [(x, z, along_x, along_z), (z, x, along_z, along_x)]

    def rows(ref, start, size):
        return ref.at[pl.ds(pl.multiple_of(start, 16), size), :]

    def remote(src, dst, s, r, target):
        return pltpu.make_async_remote_copy(src_ref=src, dst_ref=dst, send_sem=s, recv_sem=r,
                                            device_id={"mem": target}, device_id_type=MESH)

    def stage_1(h, d):
        a, b, one, two = axes[h]
        return remote(rows(packed, h * HALF + (a + d) % 4 * FOURTH, FOURTH), first_in.at[h, d - 1],
                      s1.at[h, d - 1], r1.at[h, d - 1], one(d))

    def stage_2(h, d):
        a, b, one, two = axes[h]
        return remote(rows(mid.at[h], (b + d) % 4 * LAST, LAST), second_in.at[h, d - 1],
                      s2.at[h, d - 1], r2.at[h, d - 1], two(d))

    def stage_3(h, d, back=0):
        a, b, one, two = axes[h]
        here = rows(gath, h * HALF + a * FOURTH + (b + back) % 4 * LAST, LAST)
        return remote(here, here, s3.at[h, d - 1], r3.at[h, d - 1], two(d))

    def stage_4(h, d, back=0):
        a, b, one, two = axes[h]
        here = rows(gath, h * HALF + (a + back) % 4 * FOURTH, FOURTH)
        return remote(here, here, s4.at[h, d - 1], r4.at[h, d - 1], one(d))

    def value(ref):
        return ref[...].astype(jnp.float32)

    for d in (2, 1, 3):
        for h in range(2):
            stage_1(h, d).start()
    for h in range(2):
        a, b, one, two = axes[h]
        for d in range(1, 4):
            stage_1(h, d).wait_recv()
        mid[h] = narrow(value(rows(packed, h * HALF + a * FOURTH, FOURTH))
                        + value(first_in.at[h, 0]) + value(first_in.at[h, 1]) + value(first_in.at[h, 2]))
        for d in (2, 1, 3):
            stage_2(h, d).start()
    for h in range(2):
        a, b, one, two = axes[h]
        for d in range(1, 4):
            stage_2(h, d).wait_recv()
        start = pl.multiple_of(h * HALF + a * FOURTH + b * LAST, 16)
        gath[pl.ds(start, LAST), :] = narrow(value(rows(mid.at[h], b * LAST, LAST))
                                             + value(second_in.at[h, 0]) + value(second_in.at[h, 1]) + value(second_in.at[h, 2]))
        for d in (2, 1, 3):
            stage_3(h, d).start()
    for h in range(2):
        for d in range(1, 4):
            stage_3(h, d, -d + 4).wait_recv()
        for d in (2, 1, 3):
            stage_4(h, d).start()
    for h in range(2):
        for d in range(1, 4):
            stage_4(h, d, -d + 4).wait_recv()

    def part(n):
        return gath[n * BLOCK:(n + 1) * BLOCK, :]

    for j in range(SLOTS // BLOCK):
        total = None
        for i in range(SLOTS // BLOCK):
            mine = wt[:, i * BLOCK:(i + 1) * BLOCK]
            one = dot(mine, part(PAIRS.index((i, j)))) if i <= j else dot_t(mine, part(PAIRS.index((j, i))))
            total = one if total is None else total + one
        turned[:, j * BLOCK:(j + 1) * BLOCK] = narrow(total)
    for n, (i, j) in enumerate(QUAD_PAIRS):
        gram[n] = narrow(dot_t(turned[i * BLOCK:(i + 1) * BLOCK, :], wt[j * BLOCK:(j + 1) * BLOCK, :]))

    total = None
    for q, factor in enumerate(merged_factors(lambda i, j: gram[QUAD_PAIRS.index((i, j))])):
        high = narrow(factor)
        here = wt[q * BLOCK:(q + 1) * BLOCK, :]
        one = dot(high, here) + dot(factor - high.astype(jnp.float32), here)
        total = one if total is None else total + one
    coef[...] = narrow(total)

    @pl.loop(0, CHUNKS)
    def _(q):
        out[:, pl.ds(pl.multiple_of(q * W, W), W)] = narrow(dot(coef[...], res[q]))

    @pl.loop(1, N_MEM)
    def _(o):
        meta_copy(o, mem).wait_send()

    for copy in y_copies(smeta, rmeta, ys.at[last], yr.at[last]):
        copy.wait_send()

    @pl.loop(0, CHUNKS)
    def _(q):
        @pl.loop(1, N_MEM)
        def _(o):
            image_copy(q, o, mem).wait_send()

        for copy in y_copies(send.at[q], recv.at[q], ys.at[q], yr.at[q]):
            copy.wait_send()

    for h in range(2):
        for d in range(1, 4):
            for stage in (stage_1, stage_2, stage_3, stage_4):
                stage(h, d).wait_send()


def whole(images, owner, bins, defocus, projections, weight, spread):
    vmem = pl.BlockSpec(memory_space=pltpu.VMEM)
    hbm = pl.BlockSpec(memory_space=pl.ANY)
    bf, f32 = jnp.bfloat16, jnp.float32
    dma = pltpu.SemaphoreType.DMA
    return pl.pallas_call(
        kernel,
        out_shape=jax.ShapeDtypeStruct((RANK, WIDTH), bf),
        in_specs=[hbm, vmem, vmem, vmem, hbm, vmem, vmem],
        out_specs=vmem,
        scratch_shapes=[
            pltpu.VMEM((CHUNKS, COLS, W), bf),
            pltpu.VMEM((P_DEV, 128), bf),
            pltpu.VMEM((COLS, 128), bf),
            pltpu.VMEM((SLOTS, COLS), bf),
            pltpu.VMEM((CHUNKS, SLOTS, W), bf),
            pltpu.VMEM((CHUNKS, SLOTS, W), bf),
            pltpu.VMEM((SLOTS, 128), bf),
            pltpu.VMEM((SLOTS, 128), bf),
            pltpu.VMEM((8, WIDTH), bf),
            pltpu.VMEM((ROWS, SLOTS), bf),
            pltpu.VMEM((SLOTS, 128), f32),
            pltpu.VMEM((SLOTS, 128), bf),
            pltpu.VMEM((CHUNKS, 8, W), f32),
            pltpu.VMEM((SLOTS, W), bf),
            pltpu.VMEM((CHUNKS, SLOTS, W), bf),
            pltpu.VMEM((len(PAIRS), BLOCK, BLOCK), f32),
            pltpu.VMEM((2 * HALF, BLOCK), bf),
            pltpu.VMEM((2, 3, FOURTH, BLOCK), bf),
            pltpu.VMEM((2, FOURTH, BLOCK), bf),
            pltpu.VMEM((2, 3, LAST, BLOCK), bf),
            pltpu.VMEM((2 * HALF, BLOCK), bf),
            pltpu.VMEM((ROWS, SLOTS), bf),
            pltpu.VMEM((len(QUAD_PAIRS), BLOCK, BLOCK), bf),
            pltpu.VMEM((RANK, SLOTS), bf),
            dma((CHUNKS, N_MEM)), dma((CHUNKS, N_MEM)), dma((N_MEM,)), dma((N_MEM,)),
            dma((CHUNKS + 1, N_CLS)), dma((CHUNKS + 1, N_CLS)), dma,
        ] + [dma((2, 3))] * 8,
        compiler_params=pltpu.CompilerParams(collective_id=0, has_side_effects=True, vmem_limit_bytes=60 * 1024 * 1024),
        name="basis",
    )(images, owner, bins, defocus, projections, weight, spread)


def spread_matrix():
    column = np.arange(SLOTS)
    slot = column // PART * CAP + column % CAP
    return (np.arange(N_CLS * CAP)[:, None] == slot[None, :]).astype(np.float32)


def body(images, owner_group, bin_in_group, defocus, projections, sketch_weight):
    spread = jnp.asarray(spread_matrix(), dtype=jnp.bfloat16)
    bins = bin_in_group.reshape(1, P_DEV)
    focus = defocus.reshape(1, P_DEV)
    owner = owner_group.reshape(1, P_DEV)
    return whole(images, owner, bins, focus, projections, sketch_weight.T, spread)[None]


def solution(mesh):
    in_specs = (
        P(("cls", "mem"), None),
        P(("cls", "mem"), None),
        P(("cls", "mem")),
        P(("cls", "mem")),
        P("cls", None),
        P(),
    )
    out_specs = P("cls", None, "mem")
    return jax.shard_map(body, mesh=mesh, in_specs=in_specs, out_specs=out_specs, check_vma=False)
```

```python
import functools
import math

import jax
import jax.numpy as jnp
import numpy as np
from jax import lax
from jax.experimental import pallas as pl
from jax.experimental.pallas import tpu as pltpu
from jax.sharding import PartitionSpec as P

SIDE = 256
CAP = 6
N_CLS = 8
N_MEM = 16
RANK = 64
P_DEV = 24
P_PAD = 32
PIX = 65536
WIDTH = PIX // N_MEM
CHUNKS = 8
W = WIDTH // CHUNKS
PART = N_MEM * CAP
SLOTS = N_CLS * PART
ROWS = N_MEM * RANK
COLS = N_MEM * P_PAD
BLOCK = 256
PAIRS = [(i, j) for i in range(SLOTS // BLOCK) for j in range(i, SLOTS // BLOCK)]
QUADS = ROWS // BLOCK
PIECES = 2
HALF = len(PAIRS) * BLOCK
SHARE = HALF // PIECES
FOURTH = SHARE // 4
LAST = FOURTH // 4
MESH = pl.DeviceIdType.MESH


def sine_terms():
    nodes = np.cos(np.pi * (np.arange(400) + 0.5) / 400) * 0.5
    basis = np.stack([nodes ** (2 * i + 1) for i in range(6)], axis=1)
    wanted = -math.sqrt(1.01) * np.sin(2 * np.pi * nodes)
    return [float(v) for v in np.linalg.lstsq(basis, wanted, rcond=None)[0]]


SINE = sine_terms()
ROUND = 12582912.0
STRIP = 16


def narrow(value):
    return value.astype(jnp.bfloat16)


def dot(a, b):
    return jnp.dot(narrow(a), narrow(b), preferred_element_type=jnp.float32)


def dot_t(a, b):
    return lax.dot_general(narrow(a), narrow(b), (((1,), (1,)), ((), ())), preferred_element_type=jnp.float32)


def normalise(grams):
    n = grams[0].shape[0]
    row = lax.broadcasted_iota(jnp.int32, (n, n), 0)
    col = lax.broadcasted_iota(jnp.int32, (n, n), 1)
    same = lax.shift_right_logical(row, 6) == lax.shift_right_logical(col, 6)
    diag = [jnp.sum(jnp.where(row == col, gram, 0.0), axis=0, keepdims=True) for gram in grams]
    if n == RANK:
        total = [jnp.sum(d, axis=1, keepdims=True) + 1e-06 for d in diag]
        g = [gram / t for gram, t in zip(grams, total)]
    else:
        total = [jnp.sum(jnp.where(same, d, 0.0), axis=1, keepdims=True) + 1e-06 for d in diag]
        g = [jnp.where(same, gram, 0.0) / t for gram, t in zip(grams, total)]
    g2 = [dot(a, a) for a in g]
    high = [dot(b, -0.5625 * a + 0.0625 * b) for a, b in zip(g, g2)]
    rest = [-2.4375 * a + 1.6875 * b + c for a, b, c in zip(g, g2, high)]
    return rest, [jnp.sqrt(float(PIX) / t) for t in total]


def advance(turned, factors):
    grams = [dot_t(t, f) for t, f in zip(turned, factors)]
    rest, scale = normalise(grams)
    more = [dot(r, f) for r, f in zip(rest, factors)]
    return [s * (2.25 * f + m) for s, f, m in zip(scale, factors, more)]


def merged(weights, slots, quad_gram):
    two = 2 * RANK
    row = lax.broadcasted_iota(jnp.int32, (two, two), 0)
    col = lax.broadcasted_iota(jnp.int32, (two, two), 1)
    ident = jnp.where(row == col, 1.0, 0.0)
    pairs = [quad_gram(q)[a:a + two, a:a + two] for q in range(QUADS) for a in range(0, BLOCK, two)]
    rest, scale = normalise([p.astype(jnp.float32) for p in pairs])
    chain = [s * (2.25 * ident + r) for s, r in zip(scale, rest)]
    chain = [c[:RANK] + c[RANK:] for c in chain]
    chain = advance([dot(c, p) for c, p in zip(chain, pairs)], chain)
    chain = [jnp.concatenate([chain[2 * q], chain[2 * q + 1]], axis=1) for q in range(QUADS)]
    chain = advance([dot(c, quad_gram(q)) for q, c in enumerate(chain)], chain)
    high = [narrow(c) for c in chain]
    low = [c - h.astype(jnp.float32) for c, h in zip(chain, high)]
    spread = [dot(high[q], weights(q)) + dot(low[q], weights(q)) for q in range(QUADS)]
    factor = jnp.concatenate([spread[q] + spread[q + 1] for q in range(0, QUADS, 2)], axis=0)
    while True:
        turned = jnp.concatenate([slots(factor, j) for j in range(SLOTS // BLOCK)], axis=1)
        factor = advance([turned], [factor])[0]
        if factor.shape[0] == RANK:
            return factor
        half = factor.shape[0] // 2
        factor = factor[:half] + factor[half:]


def kernel(images, owner, bins, defocus, proj, weight, spread, out, x_buf, m_own, m_buf, sel, send, recv, smeta, rmeta,
           pj, wt, focus, table, grid_q, chosen, res, acc, packed, first_in, mid, second_in, gath, full, turned, gram, coef,
           xs, xr, ms, mr, ys, yr, pm, s1, r1, s2, r2, s3, r3, s4, r4):
    cls = lax.axis_index("cls")
    mem = lax.axis_index("mem")
    y, core = cls // 2, cls % 2
    up, down, far = (y + 1) % 4, (y + 3) % 4, (y + 2) % 4
    z, x = mem // 4, mem % 4

    barrier = pltpu.get_barrier_semaphore()

    def peer(o):
        return ((z + o // 4) % 4) * 4 + (x + o % 4) % 4

    x_buf[...] = jnp.zeros_like(x_buf)
    m_buf[...] = jnp.zeros_like(m_buf)

    @pl.loop(1, N_MEM)
    def _(o):
        pl.semaphore_signal(barrier, inc=1, device_id={"mem": peer(o)}, device_id_type=MESH)

    others = [far * 2, far * 2 + 1, up * 2, down * 2 + 1, up * 2 + 1, down * 2, y * 2 + 1 - core]
    for other in others:
        pl.semaphore_signal(barrier, inc=1, device_id={"cls": other}, device_id_type=MESH)


    lane = lax.broadcasted_iota(jnp.int32, (P_DEV, 128), 1)
    row = lax.broadcasted_iota(jnp.int32, (P_DEV, P_DEV), 0)
    col = lax.broadcasted_iota(jnp.int32, (P_DEV, P_DEV), 1)
    def upright(values):
        return jnp.sum(jnp.where(row == col, values.astype(jnp.float32), 0.0), axis=1, keepdims=True)

    who = upright(owner[...])
    onehot = jnp.where(lane.astype(jnp.float32) == who, 1.0, 0.0)
    before = dot(jnp.where(col < row, 1.0, 0.0), onehot)
    rank = jnp.sum(onehot * before, axis=1, keepdims=True)
    meta = jnp.where(lane == 0, upright(defocus[...]), 0.0)
    meta = jnp.where(lane == 1, upright(bins[...]), meta)
    meta = jnp.where(lane == 2, 1.0, meta)
    m_own[...] = narrow(jnp.where(lane == 3, CAP * who + rank + 1.0, meta))
    pl.semaphore_wait(barrier, N_MEM - 1 + len(others))

    def rows_of(ref, member):
        return ref.at[pl.ds(pl.multiple_of(member * P_PAD, P_PAD), P_DEV), :]

    def meta_copy(o, owner):
        return pltpu.make_async_remote_copy(
            src_ref=m_own, dst_ref=rows_of(m_buf, owner), send_sem=ms.at[o], recv_sem=mr.at[owner],
            device_id={"mem": peer(o)}, device_id_type=MESH)

    def image_part(q, target):
        return images.at[:, pl.ds(pl.multiple_of(target * WIDTH + q * W, W), W)]

    def image_copy(q, o, owner):
        return pltpu.make_async_remote_copy(
            src_ref=image_part(q, peer(o)), dst_ref=rows_of(x_buf.at[q], owner),
            send_sem=xs.at[q, o], recv_sem=xr.at[q, owner],
            device_id={"mem": peer(o)}, device_id_type=MESH)

    def own_image(q):
        return pltpu.make_async_copy(image_part(q, mem), rows_of(x_buf.at[q], mem), xs.at[q, 0])

    own_meta = pltpu.make_async_copy(m_own, rows_of(m_buf, mem), ms.at[0])
    own_meta.start()

    @pl.loop(1, N_MEM)
    def _(o):
        meta_copy(o, mem).start()

    @pl.loop(0, CHUNKS)
    def _(q):
        own_image(q).start()

        @pl.loop(1, N_MEM)
        def _(o):
            image_copy(q, o, mem).start()

    own_proj = pltpu.make_async_copy(proj.at[:, pl.ds(pl.multiple_of(mem * WIDTH, WIDTH), WIDTH)], pj, pm)
    own_proj.start()

    wide = lax.dot_general(weight[...], spread[...], (((0,), (0,)), ((), ())), preferred_element_type=jnp.float32)
    column = lax.broadcasted_iota(jnp.int32, (RANK, SLOTS), 1).astype(jnp.float32)
    local = column - PART * jnp.floor((column + 0.5) * (1.0 / PART))
    holder = jnp.floor((local + 0.5) * (1.0 / CAP))
    for m in range(N_MEM):
        wt[m * RANK:(m + 1) * RANK, :] = jnp.where(holder == float(m), wide, 0.0).astype(jnp.bfloat16)

    @pl.loop(0, CHUNKS)
    def _(q):
        place = mem * WIDTH + q * W + lax.broadcasted_iota(jnp.int32, (8, W), 1)
        col = place & (SIDE - 1)
        row = lax.shift_right_logical(place, 8)
        fx = jnp.where(col < SIDE // 2, col, col - SIDE).astype(jnp.float32) * (1.0 / SIDE)
        fy = jnp.where(row < SIDE // 2, row, row - SIDE).astype(jnp.float32) * (1.0 / SIDE)
        grid_q[q] = (fx * fx + fy * fy) * (160.0 / (2 * math.pi))

    acc[...] = jnp.zeros_like(acc)

    own_meta.wait()

    @pl.loop(1, N_MEM)
    def _(o):
        owner = peer(N_MEM - o)
        meta_copy(o, peer(o)).wait_recv()

    lane = lax.broadcasted_iota(jnp.int32, (8, 128), 1)
    third = jnp.where(lane == 3, 1.0, 0.0).astype(jnp.bfloat16)
    code = lax.dot_general(third, m_buf[...], (((1,), (1,)), ((), ())), preferred_element_type=jnp.float32)
    which = lax.shift_right_logical(lax.broadcasted_iota(jnp.int32, (1, COLS), 1), 5).astype(jnp.float32)
    code = code[0:1, :] + 64.0 * which
    item = lax.broadcasted_iota(jnp.int32, (PART, COLS), 0).astype(jnp.float32)
    whose = jnp.floor((item + 0.5) * (1.0 / CAP))
    base = whose * 64.0 + (item - CAP * whose) + 1.0 - code
    for c in range(N_CLS):
        sel[c * PART:(c + 1) * PART, :] = jnp.where(base == -float(c * CAP), 1.0, 0.0).astype(jnp.bfloat16)

    def part_of(ref, group):
        return ref.at[pl.ds(pl.multiple_of(group * PART, PART), PART), :]

    def y_copies(src, dst, sems, rsems):
        here = part_of(dst, cls)
        return [pltpu.make_async_remote_copy(
            src_ref=part_of(src, other), dst_ref=here, send_sem=sems.at[i], recv_sem=rsems.at[cls],
            device_id={"cls": other}, device_id_type=MESH) for i, other in enumerate(others)]

    def y_own(src, dst, rsems):
        return pltpu.make_async_copy(part_of(src, cls), part_of(dst, cls), rsems.at[cls])

    def arrivals(dst, sems, rsems):
        for source in others:
            pltpu.make_async_remote_copy(
                src_ref=part_of(dst, source), dst_ref=part_of(dst, source), send_sem=sems.at[0], recv_sem=rsems.at[source],
                device_id={"cls": source}, device_id_type=MESH).wait_recv()

    last = CHUNKS
    smeta[...] = jnp.dot(sel[...], m_buf[...], preferred_element_type=jnp.float32).astype(jnp.bfloat16)
    for copy in y_copies(smeta, rmeta, ys.at[last], yr.at[last]):
        copy.start()
    y_own(smeta, rmeta, yr.at[last]).start()

    def sort(q):
        own_image(q).wait()

        @pl.loop(1, N_MEM)
        def _(o):
            image_copy(q, o, peer(o)).wait_recv()

        send[q] = jnp.dot(sel[...], x_buf[q], preferred_element_type=jnp.float32).astype(jnp.bfloat16)
        for copy in y_copies(send.at[q], recv.at[q], ys.at[q], yr.at[q]):
            copy.start()
        y_own(send.at[q], recv.at[q], yr.at[q]).start()

    def prepare():
        y_own(smeta, rmeta, yr.at[last]).wait()
        arrivals(rmeta, ys.at[last], yr.at[last])
        pick = lax.broadcasted_iota(jnp.int32, (128, 128), 0)
        m = rmeta[...]
        def lanes(i):
            return jnp.dot(m, jnp.where(pick == i, 1.0, 0.0).astype(jnp.bfloat16), preferred_element_type=jnp.float32)
        focus[...] = lanes(0)
        at = lax.broadcasted_iota(jnp.int32, (SLOTS, 128), 1).astype(jnp.float32)
        table[...] = jnp.where((lanes(1) == at) & (lanes(2) == 1.0), 1.0, 0.0).astype(jnp.bfloat16)
        own_proj.wait()

    def consume(q):
        y_own(send.at[q], recv.at[q], yr.at[q]).wait()
        arrivals(recv.at[q], ys.at[q], yr.at[q])
        projected = pj[:, pl.ds(pl.multiple_of(q * W, W), W)]
        chosen[...] = jnp.dot(table[:, 0:8], projected, preferred_element_type=jnp.float32).astype(jnp.bfloat16)

        @pl.loop(0, SLOTS // STRIP, unroll=2)
        def _(i):
            r = pl.ds(pl.multiple_of(i * STRIP, STRIP), STRIP)
            f = focus[r, :]
            for l in range(W // 128):
                cols = slice(l * 128, (l + 1) * 128)
                g = grid_q[q, :, cols]
                turn = f * jnp.concatenate([g] * (STRIP // 8), axis=0) + math.atan(0.1) / (2 * math.pi)
                turn = turn - ((turn + ROUND) - ROUND)
                sq = turn * turn
                value = SINE[5]
                for term in SINE[4::-1]:
                    value = value * sq + term
                ctf = value * turn
                got = recv[q, r, cols].astype(jnp.float32)
                res[q, r, cols] = (got - ctf * chosen[r, cols].astype(jnp.float32)).astype(jnp.bfloat16)

        for n, (i, j) in enumerate(PAIRS):
            acc[n] += dot_t(res[q, i * BLOCK:(i + 1) * BLOCK, :], res[q, j * BLOCK:(j + 1) * BLOCK, :])

    @pl.loop(0, CHUNKS + 2)
    def _(t):
        @pl.when(t < CHUNKS)
        def _():
            sort(t)

        @pl.when(t == 2)
        def _():
            prepare()

        @pl.when(t >= 2)
        def _():
            consume(t - 2)

    for n in range(len(PAIRS)):
        for side in range(2):
            packed[(2 * n + side) * BLOCK:(2 * n + side + 1) * BLOCK, :] = narrow(acc[n, :, side * 128:(side + 1) * 128])

    def along_x(d):
        return z * 4 + (x + d) % 4

    def along_z(d):
        return ((z + d) % 4) * 4 + x

    axes = [(x, z, along_x, along_z), (z, x, along_z, along_x)]
    lines = [(h, k) for k in range(PIECES) for h in range(2)]

    def rows(ref, start, size):
        return ref.at[pl.ds(pl.multiple_of(start, 16), size), :]

    def remote(src, dst, s, r, target):
        return pltpu.make_async_remote_copy(src_ref=src, dst_ref=dst, send_sem=s, recv_sem=r,
                                            device_id={"mem": target}, device_id_type=MESH)

    def stage_1(h, k, d):
        a, b, one, two = axes[h]
        return remote(rows(packed, h * HALF + k * SHARE + (a + d) % 4 * FOURTH, FOURTH), first_in.at[h, k, d - 1],
                      s1.at[h, k, d - 1], r1.at[h, k, d - 1], one(d))

    def stage_2(h, k, d):
        a, b, one, two = axes[h]
        return remote(rows(mid.at[h, k], (b + d) % 4 * LAST, LAST), second_in.at[h, k, d - 1],
                      s2.at[h, k, d - 1], r2.at[h, k, d - 1], two(d))

    def stage_3(h, k, d, back=0):
        a, b, one, two = axes[h]
        here = rows(gath, h * HALF + k * SHARE + a * FOURTH + (b + back) % 4 * LAST, LAST)
        return remote(here, here, s3.at[h, k, d - 1], r3.at[h, k, d - 1], two(d))

    def stage_4(h, k, d, back=0):
        a, b, one, two = axes[h]
        here = rows(gath, h * HALF + k * SHARE + (a + back) % 4 * FOURTH, FOURTH)
        return remote(here, here, s4.at[h, k, d - 1], r4.at[h, k, d - 1], one(d))

    def value(ref):
        return ref[...].astype(jnp.float32)

    for h, k in lines:
        for d in (2, 1, 3):
            stage_1(h, k, d).start()
    for h, k in lines:
        a, b, one, two = axes[h]
        for d in range(1, 4):
            stage_1(h, k, d).wait_recv()
        mid[h, k] = narrow(value(rows(packed, h * HALF + k * SHARE + a * FOURTH, FOURTH))
                           + value(first_in.at[h, k, 0]) + value(first_in.at[h, k, 1]) + value(first_in.at[h, k, 2]))
        for d in (2, 1, 3):
            stage_2(h, k, d).start()
    for h, k in lines:
        a, b, one, two = axes[h]
        for d in range(1, 4):
            stage_2(h, k, d).wait_recv()
        start = pl.multiple_of(h * HALF + k * SHARE + a * FOURTH + b * LAST, 16)
        gath[pl.ds(start, LAST), :] = narrow(value(rows(mid.at[h, k], b * LAST, LAST)) + value(second_in.at[h, k, 0])
                                             + value(second_in.at[h, k, 1]) + value(second_in.at[h, k, 2]))
        for d in (2, 1, 3):
            stage_3(h, k, d).start()
    for h, k in lines:
        for d in range(1, 4):
            stage_3(h, k, d, -d + 4).wait_recv()
        for d in (2, 1, 3):
            stage_4(h, k, d).start()
    for h, k in lines:
        for d in range(1, 4):
            stage_4(h, k, d, -d + 4).wait_recv()

    for n in range(len(PAIRS)):
        for side in range(2):
            full[n, :, side * 128:(side + 1) * 128] = gath[(2 * n + side) * BLOCK:(2 * n + side + 1) * BLOCK, :]

    def slots(value, j):
        total = None
        for i in range(SLOTS // BLOCK):
            mine = value[:, i * BLOCK:(i + 1) * BLOCK]
            one = dot(mine, full[PAIRS.index((i, j))]) if i <= j else dot_t(mine, full[PAIRS.index((j, i))])
            total = one if total is None else total + one
        return total

    for j in range(SLOTS // BLOCK):
        turned[:, j * BLOCK:(j + 1) * BLOCK] = narrow(slots(wt[...], j))

    def rows_of_quad(ref, q):
        return ref[q * BLOCK:(q + 1) * BLOCK, :]

    for q in range(QUADS):
        gram[q] = narrow(dot_t(rows_of_quad(turned, q), rows_of_quad(wt, q)))
    coef[...] = narrow(merged(lambda q: rows_of_quad(wt, q), slots, lambda q: gram[q]))

    @pl.loop(0, CHUNKS)
    def _(q):
        out[:, pl.ds(pl.multiple_of(q * W, W), W)] = narrow(dot(coef[...], res[q]))

    @pl.loop(1, N_MEM)
    def _(o):
        meta_copy(o, mem).wait_send()

    for copy in y_copies(smeta, rmeta, ys.at[last], yr.at[last]):
        copy.wait_send()

    @pl.loop(0, CHUNKS)
    def _(q):
        @pl.loop(1, N_MEM)
        def _(o):
            image_copy(q, o, mem).wait_send()

        for copy in y_copies(send.at[q], recv.at[q], ys.at[q], yr.at[q]):
            copy.wait_send()

    for h, k in lines:
        for d in range(1, 4):
            for stage in (stage_1, stage_2, stage_3, stage_4):
                stage(h, k, d).wait_send()


def whole(images, owner, bins, defocus, projections, weight, spread):
    vmem = pl.BlockSpec(memory_space=pltpu.VMEM)
    hbm = pl.BlockSpec(memory_space=pl.ANY)
    bf, f32 = jnp.bfloat16, jnp.float32
    dma = pltpu.SemaphoreType.DMA
    return pl.pallas_call(
        kernel,
        out_shape=jax.ShapeDtypeStruct((RANK, WIDTH), bf),
        in_specs=[hbm, vmem, vmem, vmem, hbm, vmem, vmem],
        out_specs=vmem,
        scratch_shapes=[
            pltpu.VMEM((CHUNKS, COLS, W), bf),
            pltpu.VMEM((P_DEV, 128), bf),
            pltpu.VMEM((COLS, 128), bf),
            pltpu.VMEM((SLOTS, COLS), bf),
            pltpu.VMEM((CHUNKS, SLOTS, W), bf),
            pltpu.VMEM((CHUNKS, SLOTS, W), bf),
            pltpu.VMEM((SLOTS, 128), bf),
            pltpu.VMEM((SLOTS, 128), bf),
            pltpu.VMEM((8, WIDTH), bf),
            pltpu.VMEM((ROWS, SLOTS), bf),
            pltpu.VMEM((SLOTS, 128), f32),
            pltpu.VMEM((SLOTS, 128), bf),
            pltpu.VMEM((CHUNKS, 8, W), f32),
            pltpu.VMEM((SLOTS, W), bf),
            pltpu.VMEM((CHUNKS, SLOTS, W), bf),
            pltpu.VMEM((len(PAIRS), BLOCK, BLOCK), f32),
            pltpu.VMEM((2 * HALF, 128), bf),
            pltpu.VMEM((2, PIECES, 3, FOURTH, 128), bf),
            pltpu.VMEM((2, PIECES, FOURTH, 128), bf),
            pltpu.VMEM((2, PIECES, 3, LAST, 128), bf),
            pltpu.VMEM((2 * HALF, 128), bf),
            pltpu.VMEM((len(PAIRS), BLOCK, BLOCK), bf),
            pltpu.VMEM((ROWS, SLOTS), bf),
            pltpu.VMEM((QUADS, BLOCK, BLOCK), bf),
            pltpu.VMEM((RANK, SLOTS), bf),
            dma((CHUNKS, N_MEM)), dma((CHUNKS, N_MEM)), dma((N_MEM,)), dma((N_MEM,)),
            dma((CHUNKS + 1, N_CLS)), dma((CHUNKS + 1, N_CLS)), dma,
        ] + [dma((2, PIECES, 3))] * 8,
        compiler_params=pltpu.CompilerParams(collective_id=0, has_side_effects=True, vmem_limit_bytes=60 * 1024 * 1024),
        name="basis",
    )(images, owner, bins, defocus, projections, weight, spread)


def spread_matrix():
    column = np.arange(SLOTS)
    slot = column // PART * CAP + column % CAP
    return (np.arange(N_CLS * CAP)[:, None] == slot[None, :]).astype(np.float32)


def body(images, owner_group, bin_in_group, defocus, projections, sketch_weight):
    spread = jnp.asarray(spread_matrix(), dtype=jnp.bfloat16)
    bins = bin_in_group.reshape(1, P_DEV)
    focus = defocus.reshape(1, P_DEV)
    owner = owner_group.reshape(1, P_DEV)
    return whole(images, owner, bins, focus, projections, sketch_weight.T, spread)[None]


def solution(mesh):
    in_specs = (
        P(("cls", "mem"), None),
        P(("cls", "mem"), None),
        P(("cls", "mem")),
        P(("cls", "mem")),
        P("cls", None),
        P(),
    )
    out_specs = P("cls", None, "mem")
    return jax.shard_map(body, mesh=mesh, in_specs=in_specs, out_specs=out_specs, check_vma=False)
```
